512 devices in a mesh: gx: 16 (over z, core), gy: 32 (over y, x).
Axes of the slice: x: 4, y: 8, z: 8, core: 2. Of those that a mesh axis runs over, the one named last changes fastest.
Arguments:
- positions: float32 [3, 16, 32, 4096], P(None, 'gx', 'gy'), may hold values from 0 to 2
- velocities: float32 [3, 16, 32, 4096], P(None, 'gx', 'gy'), may hold values from -6 to 6
- mass: float32 [16, 32, 4096], P('gx', 'gy'), may hold values from 0.05 to 0.3
- stiffness: float32 [16, 32, 4096], P('gx', 'gy'), may hold values from 0.5 to 8
- counts: int32 [16, 32, 32], P('gx', 'gy'), may hold values from 32 to 128
- pairs: int32 [65536, 2], P(('gx', 'gy')), may hold values from 0 to 16383, as said below
- pair_count: int32 [512], P(('gx', 'gy')), may hold values from 32 to 128, as said below
Outputs:
- new_positions: float32 [3, 16, 32, 4096], P(None, 'gx', 'gy')
- new_velocities: float32 [3, 16, 32, 4096], P(None, 'gx', 'gy')
- density: float32 [16, 32, 4096], P('gx', 'gy')
The draws below stay inside these ranges and needn't reach their ends.
Inputs may be any that keep to these rules, and one draw needn't show every extreme that they name: `pairs`: box d's list is rows d * 128 to (d + 1) * 128 - 1, box d being (d // 32, d % 32). Its first 32 rows pair each of the box's own tiles with itself, in order. In every other row the first tile lies in a box with the same gy index and a gx index at most one away, the second tile in a box with the same gx index and a gy index at most one away. Rows may repeat. `pair_count`: some box has 128 live rows in every draw.
All inputs are finite; a program needn't handle non-finite values.
Results may differ from the reference program's by a relative error of at most 0.0001.
Values sent between devices are 32-bit elements; how exact they have to be, the bound alone decides.
A program may use at most 64 MiB of HBM per device.

```python
import math
import jax
import jax.numpy as jnp
from jax import lax

TILE = 128
TILES_DEV = 32
PAIRS_MAX = 128
SLOTS = 4096
N_GX = 16
N_GY = 32


def draw_pairs(key, part):
    boxes = N_GX * N_GY
    keys = jax.random.split(jax.random.fold_in(key, 11), 4)
    box_index = jnp.arange(boxes, dtype=jnp.int32)
    box_row = box_index // N_GY
    box_column = box_index % N_GY
    extra = PAIRS_MAX - TILES_DEV
    step_row = jax.random.randint(keys[0], (boxes, extra), -1, 2)
    step_column = jax.random.randint(keys[1], (boxes, extra), -1, 2)
    first_row = jnp.clip(box_row[:, None] + step_row, 0, N_GX - 1)
    second_column = jnp.clip(box_column[:, None] + step_column, 0, N_GY - 1)
    first_slot = jax.random.randint(keys[2], (boxes, extra), 0, TILES_DEV)
    second_slot = jax.random.randint(keys[3], (boxes, extra), 0, TILES_DEV)
    first_tiles = (first_row * N_GY + box_column[:, None]) * TILES_DEV + first_slot
    second_tiles = (box_row[:, None] * N_GY + second_column) * TILES_DEV + second_slot
    own_tiles = box_index[:, None] * TILES_DEV + jnp.arange(TILES_DEV, dtype=jnp.int32)[None, :]
    first_all = jnp.concatenate([own_tiles, first_tiles], axis=1)
    second_all = jnp.concatenate([own_tiles, second_tiles], axis=1)
    return jnp.stack([first_all, second_all], axis=-1).reshape(boxes * PAIRS_MAX, 2).astype(jnp.int32)


def draw_pair_count(key, part):
    boxes = N_GX * N_GY
    keys = jax.random.split(jax.random.fold_in(key, 23), 2)
    level = jax.random.randint(keys[0], (boxes,), 0, 65)
    extra = PAIRS_MAX - TILES_DEV
    loads = TILES_DEV + extra * level * level * level // 262144
    busiest = jax.random.randint(keys[1], (), 0, boxes)
    box_index = jnp.arange(boxes, dtype=jnp.int32)
    loads = jnp.where(box_index == busiest, PAIRS_MAX, loads)
    return loads.astype(jnp.int32)


def touch_ends(result, own_key, low, largest):
    index_at = [jax.random.randint(jax.random.fold_in(own_key, axis), (), 0, length) for axis, length in enumerate(result.shape)]
    main_axis = result.shape.index(max(result.shape))
    next_to = index_at[:main_axis] + [(index_at[main_axis] + 1) % result.shape[main_axis]] + index_at[main_axis + 1:]
    return result.at[tuple(index_at)].set(low).at[tuple(next_to)].set(largest)


def block_scale(key, dims, cuts, least, top_value):
    def one(position, parts):
        heights = jax.random.uniform(jax.random.fold_in(jax.random.fold_in(key, 6), position), (parts,), jnp.float32, least / len(cuts), top_value / len(cuts))
        return jnp.repeat(jnp.exp(heights), dims[position] // parts).reshape((-1,) + (1,) * (len(dims) - position - 1))

    loudness = one(*cuts[0])
    for cut in cuts[1:]:
        loudness = loudness * one(*cut)
    return loudness


def scatter_about(stream_key, dims, spread, bound, pieces=(), kind=jnp.bfloat16):
    loudness = block_scale(stream_key, dims, pieces, -0.22, 0.18) if pieces else 1.0
    values = jax.random.normal(stream_key, dims, jnp.float32) * spread * loudness
    return jnp.minimum(jnp.maximum(values, -bound), bound).astype(kind)


def setup_inputs(seed: int = 0) -> dict:
    seeds = jax.random.split(jax.random.key(seed), 8)
    positions = jnp.clip(2.0 * jax.random.uniform(seeds[0], (3, N_GX, N_GY, SLOTS), jnp.float32) ** block_scale(seeds[0], (3, N_GX, N_GY, SLOTS), ((1, 16), (2, 32)), -0.2, 0.2), 0.0, 2.0)
    velocities = scatter_about(seeds[1], (3, N_GX, N_GY, SLOTS), 1.0, 6.0, ((1, 16), (2, 32)), jnp.float32)
    mass = jnp.clip(jnp.exp(math.log(0.3) - 1.7917595 * jax.random.uniform(seeds[2], (N_GX, N_GY, SLOTS), jnp.float32) ** block_scale(seeds[2], (N_GX, N_GY, SLOTS), ((0, 16), (1, 32)), -0.2, 0.2)), 0.05, 0.3)
    stiffness = jnp.clip(jnp.exp(math.log(8.0) - 2.7725887 * jax.random.uniform(seeds[3], (N_GX, N_GY, SLOTS), jnp.float32) ** block_scale(seeds[3], (N_GX, N_GY, SLOTS), ((0, 16), (1, 32)), -0.2, 0.2)), 0.5, 8.0)
    counts = touch_ends(jax.random.randint(seeds[4], (N_GX, N_GY, TILES_DEV), 32, 129), jax.random.fold_in(seeds[4], 1), 32, 128).astype(jnp.int32)
    pairs = draw_pairs(jax.random.fold_in(seeds[7], 71), 0)
    pair_count = draw_pair_count(jax.random.fold_in(seeds[7], 71), 0)
    return dict(positions=positions, velocities=velocities, mass=mass, stiffness=stiffness, counts=counts, pairs=pairs, pair_count=pair_count)


kernel_norm = 21.0 / (16.0 * math.pi)
viscosity = 0.1
time_step = 0.02
rest_density = 1.0

def kernel_terms(points_a, points_b):
    offset = points_a[:, :, :, None] - points_b[:, :, None, :]
    distance = jnp.sqrt(lax.optimization_barrier(jnp.sum(offset * offset, axis=0)))
    falloff = jnp.maximum(1.0 - 0.5 * distance, 0.0)
    weight = kernel_norm * falloff ** 4 * (2.0 * distance + 1.0)
    slope = -5.0 * kernel_norm * falloff ** 3
    return (offset, weight, slope)

def density_terms(points_a, points_b, mass_a, mass_b, live_rows, cross_rows):
    offset, weight, slope = kernel_terms(points_a, points_b)
    to_first = lax.optimization_barrier(jnp.sum(weight * mass_b[:, None, :], axis=2)) * live_rows[:, None]
    to_second = lax.optimization_barrier(jnp.sum(weight * mass_a[:, :, None], axis=1)) * cross_rows[:, None]
    return (to_first, to_second)

def force_terms(points_a, points_b, speed_a, speed_b, mass_a, mass_b, press_a, press_b, scale_a, scale_b, live_rows, cross_rows):
    offset, weight, slope = kernel_terms(points_a, points_b)
    push = -(press_a[:, :, None] + press_b[:, None, :])
    drag = 2.0 * viscosity / (scale_a[:, :, None] * scale_b[:, None, :])
    relative = speed_a[:, :, :, None] - speed_b[:, :, None, :]
    force = slope[None] * (push[None] * offset + drag[None] * relative)
    to_first = lax.optimization_barrier(jnp.sum(force * mass_b[None, :, None, :], axis=3)) * live_rows[None, :, None]
    to_second = -lax.optimization_barrier(jnp.sum(force * mass_a[None, :, :, None], axis=2)) * cross_rows[None, :, None]
    return (to_first, to_second)

def reference(positions, velocities, mass, stiffness, counts, pairs, pair_count):
    tile_total = N_GX * N_GY * TILES_DEV
    points = positions.reshape(3, tile_total, TILE)
    speeds = velocities.reshape(3, tile_total, TILE)
    slot_index = jnp.arange(TILE, dtype=jnp.int32)
    validity = (slot_index[None, :] < counts.reshape(tile_total, 1)).astype(jnp.float32)
    weighted = mass.reshape(tile_total, TILE) * validity
    live_flag = (jnp.arange(PAIRS_MAX, dtype=jnp.int32)[None, :] < pair_count[:, None]).astype(jnp.float32).reshape(-1)
    first_tiles = pairs[:, 0]
    second_tiles = pairs[:, 1]
    cross_flag = jnp.where(first_tiles != second_tiles, live_flag, 0.0 * live_flag)
    row_total = first_tiles.shape[0]
    block_rows = math.gcd(row_total, 256)
    block_count = row_total // block_rows
    inputs = (first_tiles.reshape(block_count, block_rows), second_tiles.reshape(block_count, block_rows), live_flag.reshape(block_count, block_rows), cross_flag.reshape(block_count, block_rows))

    def density_block(totals, block):
        first_ids, second_ids, live_rows, cross_rows = block
        to_first, to_second = density_terms(points[:, first_ids], points[:, second_ids], weighted[first_ids], weighted[second_ids], live_rows, cross_rows)
        totals = totals.at[first_ids].add(to_first).at[second_ids].add(to_second)
        return (totals, None)
    density, ignored = lax.scan(density_block, jnp.zeros((tile_total, TILE), jnp.float32), inputs)
    scale = density + 1.0 - validity
    press = stiffness.reshape(tile_total, TILE) * (density - rest_density) / (scale * scale)

    def force_block(totals, block):
        first_ids, second_ids, live_rows, cross_rows = block
        to_first, to_second = force_terms(points[:, first_ids], points[:, second_ids], speeds[:, first_ids], speeds[:, second_ids], weighted[first_ids], weighted[second_ids], press[first_ids], press[second_ids], scale[first_ids], scale[second_ids], live_rows, cross_rows)
        totals = totals.at[:, first_ids].add(to_first).at[:, second_ids].add(to_second)
        return (totals, None)
    accel, ignored = lax.scan(force_block, jnp.zeros((3, tile_total, TILE), jnp.float32), inputs)
    new_speeds = speeds + time_step * validity[None] * accel
    new_points = points + time_step * new_speeds
    return (new_points.reshape(positions.shape), new_speeds.reshape(velocities.shape), density.reshape(mass.shape))
```

```python
import functools
import math

import jax
import jax.numpy as jnp
from jax import lax
from jax.experimental import pallas as pl
from jax.experimental.pallas import tpu as pltpu
from jax.sharding import PartitionSpec as P

kernel_norm = 21.0 / (16.0 * math.pi)
viscosity = 0.1
time_step = 0.02
rest_density = 1.0

MESH = pl.DeviceIdType.MESH
OWN = 2
BOXES = 5
BESIDE = (0, 1, 3, 4)
KDEPTH = 32
FEATURES = 16
UNROLL = 4

f32, bf16 = jnp.float32, jnp.bfloat16


def split_in(value, parts):
    pieces = []
    for _ in range(parts):
        piece = value.astype(bf16)
        pieces.append(piece)
        value = value - piece.astype(f32)
    return pieces


def dot_nn(a, b):
    return lax.dot_general(a, b, (((1,), (0,)), ((), ())), preferred_element_type=f32)


def dot_nt(a, b):
    return lax.dot_general(a, b, (((1,), (1,)), ((), ())), preferred_element_type=f32)


def kernel(
    gx, gy, tiles, size, rows,
    pos, vel, mass, stiff, counts, pairs_v, pairs_s, live_s,
    accel_out, density_out,
    pm, vs, side_a, side_b, mass_rows, feats, slope, row_density, row_force, picks,
    dens_part, dens_recv, dens_total, force_part, force_recv, send_sem, recv_sem,
):
    my_x, my_y = lax.axis_index("gx"), lax.axis_index("gy")
    where_to = {
        0: (lax.rem(my_x + gx - 1, gx), my_y),
        1: (my_x, lax.rem(my_y + gy - 1, gy)),
        3: (my_x, lax.rem(my_y + 1, gy)),
        4: (lax.rem(my_x + 1, gx), my_y),
    }
    all_tiles = BOXES * tiles

    barrier = pltpu.get_barrier_semaphore()
    for b in BESIDE:
        pl.semaphore_signal(barrier, inc=1, device_id=where_to[b], device_id_type=MESH)

    row_at = lax.broadcasted_iota(jnp.int32, (tiles, tiles), 0)
    column_at = lax.broadcasted_iota(jnp.int32, (tiles, tiles), 1)
    count = jnp.sum(
        jnp.where(row_at == column_at, counts[...].astype(f32), 0.0), axis=1, keepdims=True
    )
    lane = lax.broadcasted_iota(jnp.int32, (tiles, size), 1).astype(f32)
    for c in range(3):
        pm[OWN, c] = 0.5 * (pos[c] - 1.0)
        vs[OWN, c] = vel[c]
    pm[OWN, 3] = jnp.where(lane < count, mass[...], 0.0)
    vs[OWN, 3] = stiff[...]

    pl.semaphore_wait(barrier, len(BESIDE))

    def exchange(stage, source_of, target):
        copies = {}
        for b in BESIDE:
            copies[b] = pltpu.make_async_remote_copy(
                src_ref=source_of(b),
                dst_ref=target.at[4 - b],
                send_sem=send_sem.at[stage, b],
                recv_sem=recv_sem.at[stage, 4 - b],
                device_id=where_to[b],
                device_id_type=MESH,
            )
            copies[b].start()
        return copies

    def arrived(stage, b, target):
        pltpu.make_async_remote_copy(
            src_ref=target.at[b],
            dst_ref=target.at[b],
            send_sem=send_sem.at[stage, b],
            recv_sem=recv_sem.at[stage, b],
            device_id=where_to[b],
            device_id_type=MESH,
        ).wait_recv()

    sent = []
    sent.append(exchange(0, lambda b: pm.at[OWN], pm))
    sent.append(exchange(1, lambda b: vs.at[OWN], vs))

    def at_plane(ref, plane, b):
        return ref.at[pl.ds(plane * all_tiles + b * tiles, tiles)]

    def distance_planes(b):
        ones = jnp.ones((tiles, size), f32)
        norm = jnp.zeros((tiles, size), f32)
        planes_a, planes_b = [], []
        for c in range(3):
            h = pm[b, c]
            norm = norm + h * h
            h1, h2, h3 = (p.astype(f32) for p in split_in(h, 3))
            planes_a += [-2.0 * v for v in (h1, h1, h2, h2, h1, h3)]
            planes_b += [h1, h2, h1, h2, h3, h1]
        n_parts = [p.astype(f32) for p in split_in(norm, 3)]
        planes_a += n_parts + [ones] * 3
        planes_b += [ones] * 3 + n_parts
        if b in (0, OWN, 4):
            for k, value in enumerate(planes_a):
                at_plane(side_a, k, b)[...] = value
        if b in (1, OWN, 3):
            for k, value in enumerate(planes_b):
                at_plane(side_b, k, b)[...] = value
        for k, value in enumerate(split_in(pm[b, 3], 3)):
            at_plane(mass_rows, k, b)[...] = value.astype(f32)

    def zero_planes(ref, first, last):
        ref[pl.ds(first * all_tiles, (last - first) * all_tiles)] = jnp.zeros(
            ((last - first) * all_tiles, size), f32
        )

    distance_planes(OWN)
    zero_planes(side_a, 24, KDEPTH)
    zero_planes(side_b, 24, KDEPTH)
    zero_planes(mass_rows, 3, 8)
    for part in range(3):
        zero_planes(feats, part * FEATURES + 12, (part + 1) * FEATURES)
    row_density[pl.ds(rows, tiles)] = jnp.zeros((tiles, size), f32)
    for f in range(12):
        row_force[pl.ds(f * 2 * rows + rows, tiles)] = jnp.zeros((tiles, size), f32)

    first = pairs_v[0:1, :]
    second = pairs_v[1:2, :]
    row_index = lax.broadcasted_iota(jnp.int32, (1, rows), 1)
    live = row_index < live_s[0]

    def local_first(tile):
        return (OWN + 2 * (lax.div(tile, gy * tiles) - my_x)) * tiles + lax.rem(tile, tiles)

    def local_second(tile):
        return (OWN + lax.rem(lax.div(tile, tiles), gy) - my_y) * tiles + lax.rem(tile, tiles)

    to_first = jnp.where(live, local_first(first), -1)
    to_second = jnp.where(live & (first != second), local_second(second), -1)
    tile_at = lax.broadcasted_iota(jnp.int32, (all_tiles, rows), 0)
    picks[:, 0:rows] = jnp.where(tile_at == to_first, 1.0, 0.0).astype(bf16)
    picks[:, rows : 2 * rows] = jnp.where(tile_at == to_second, 1.0, 0.0).astype(bf16)

    def tile_rows(ref, tile, count):
        return ref[pl.ds(tile, count, stride=all_tiles), :].astype(bf16)

    def twice(value):
        return jnp.concatenate([value, value], axis=1)

    def density_row(r, t1, t2, cross):
        a = tile_rows(side_a, t1, KDEPTH)
        b = tile_rows(side_b, t2, KDEPTH)
        square = lax.dot_general(a, b, (((0,), (0,)), ((), ())), preferred_element_type=f32)
        square = jnp.maximum(square, 1e-13)
        fall = jnp.maximum(1.0 - square * lax.rsqrt(square), 0.0)
        fall2 = fall * fall
        weight_hi, weight_lo = split_in(fall2 * fall2 * (5.0 - 4.0 * fall), 2)
        slope_hi, slope_lo = split_in(fall2 * fall, 2)
        slope[r, :, 0:size] = slope_hi
        slope[r, :, size : 2 * size] = slope_lo
        beside = jnp.concatenate([weight_hi, weight_lo], axis=1)
        got = dot_nt(twice(tile_rows(mass_rows, t2, 8)), beside)
        row_density[pl.ds(r, 1)] = jnp.sum(got, axis=0, keepdims=True)
        if cross:
            below = jnp.concatenate([weight_hi, weight_lo], axis=0)
            got = dot_nn(twice(tile_rows(mass_rows, t1, 8)), below)
            row_density[pl.ds(rows + r, 1)] = jnp.sum(got, axis=0, keepdims=True)

    def force_row(r, t1, t2, cross):
        both = slope[r]

        def summed(got):
            return got[0:16] + got[16:32] + got[32:48]

        got = dot_nt(twice(tile_rows(feats, t2, 3 * FEATURES)), both)
        row_force[pl.ds(r, FEATURES, stride=2 * rows), :] = summed(got)
        if cross:
            below = jnp.concatenate([both[:, 0:size], both[:, size : 2 * size]], axis=0)
            got = dot_nn(twice(tile_rows(feats, t1, 3 * FEATURES)), below)
            row_force[pl.ds(rows + r, FEATURES, stride=2 * rows), :] = summed(got)

    def own_rows(work):
        def turn(step, carry):
            for u in range(UNROLL):
                r = step * UNROLL + u
                work(r, OWN * tiles + r, OWN * tiles + r, False)
            return carry

        lax.fori_loop(0, tiles // UNROLL, turn, 0)

    def cross_rows(work):
        def turn(step, carry):
            for u in range(UNROLL):
                r = tiles + step * UNROLL + u
                t1 = jnp.clip(local_first(pairs_s[0, r]), 0, all_tiles - 1)
                t2 = jnp.clip(local_second(pairs_s[1, r]), 0, all_tiles - 1)
                work(r, t1, t2, True)
            return carry

        lax.fori_loop(0, (rows - tiles) // UNROLL, turn, 0)

    own_rows(density_row)
    for b in BESIDE:
        arrived(0, b, pm)
        distance_planes(b)
    cross_rows(density_row)

    chosen = picks[...]
    total = jnp.zeros((all_tiles, size), f32)
    for part in split_in(row_density[...], 3):
        total = total + dot_nn(chosen, part)
    dens_part[...] = (kernel_norm * total).reshape(BOXES, tiles, size)
    sent.append(exchange(2, lambda b: dens_part.at[b], dens_recv))
    density = dens_part[OWN]
    for b in BESIDE:
        arrived(2, b, dens_recv)
        density = density + dens_recv[b]
    dens_total[OWN] = density
    density_out[...] = density
    sent.append(exchange(3, lambda b: dens_total.at[OWN], dens_total))

    def pressures(b):
        density = dens_total[b]
        scale = density + 1.0 - jnp.where(pm[b, 3] > 0.0, 1.0, 0.0)
        inverse = 1.0 / scale
        press = vs[b, 3] * (density - rest_density) * inverse * inverse
        return press, inverse

    def force_planes(b):
        press, inverse = pressures(b)
        m = pm[b, 3]
        mp, mq = m * press, m * inverse
        values = [m] + [m * pm[b, c] for c in range(3)]
        values += [mp] + [mp * pm[b, c] for c in range(3)]
        values += [mq] + [mq * vs[b, c] for c in range(3)]
        for k, value in enumerate(values):
            for part, piece in enumerate(split_in(value, 3)):
                at_plane(feats, part * FEATURES + k, b)[...] = piece.astype(f32)

    force_planes(OWN)
    own_rows(force_row)
    for b in BESIDE:
        arrived(1, b, vs)
        arrived(3, b, dens_total)
        force_planes(b)
    cross_rows(force_row)

    sums = []
    for f in range(12):
        total = jnp.zeros((all_tiles, size), f32)
        for part in split_in(row_force[pl.ds(f * 2 * rows, 2 * rows)], 3):
            total = total + dot_nn(chosen, part)
        sums.append(total)
    for b in range(BOXES):
        press, inverse = pressures(b)
        s = [v[b * tiles : (b + 1) * tiles] for v in sums]
        for c in range(3):
            h, v = pm[b, c], vs[b, c]
            push = press * (h * s[0] - s[1 + c]) + h * s[4] - s[5 + c]
            drag = inverse * (v * s[8] - s[9 + c])
            force_part[b, c] = (5.0 * kernel_norm) * (2.0 * push - (2.0 * viscosity) * drag)
    sent.append(exchange(4, lambda b: force_part.at[b], force_recv))
    accel = force_part[OWN]
    for b in BESIDE:
        arrived(4, b, force_recv)
        accel = accel + force_recv[b]
    accel_out[...] = accel * jnp.where(pm[OWN, 3] > 0.0, 1.0, 0.0)[None]

    for copies in sent:
        for b in BESIDE:
            copies[b].wait_send()


def body(gx, gy, positions, velocities, mass, stiffness, counts, pairs, pair_count):
    tiles = counts.shape[2]
    size = positions.shape[3] // tiles
    rows = pairs.shape[0]
    all_tiles = BOXES * tiles
    points = positions.reshape(3, tiles, size)
    speeds = velocities.reshape(3, tiles, size)
    turned = pairs.T
    vmem = pl.BlockSpec(memory_space=pltpu.VMEM)
    smem = pl.BlockSpec(memory_space=pltpu.SMEM)
    accel, density = pl.pallas_call(
        functools.partial(kernel, gx, gy, tiles, size, rows),
        out_shape=(
            jax.ShapeDtypeStruct((3, tiles, size), f32),
            jax.ShapeDtypeStruct((tiles, size), f32),
        ),
        in_specs=[vmem] * 6 + [smem] * 2,
        out_specs=(vmem, vmem),
        scratch_shapes=[
            pltpu.VMEM((BOXES, 4, tiles, size), f32),
            pltpu.VMEM((BOXES, 4, tiles, size), f32),
            pltpu.VMEM((KDEPTH * all_tiles, size), f32),
            pltpu.VMEM((KDEPTH * all_tiles, size), f32),
            pltpu.VMEM((8 * all_tiles, size), f32),
            pltpu.VMEM((3 * FEATURES * all_tiles, size), f32),
            pltpu.VMEM((rows, size, 2 * size), bf16),
            pltpu.VMEM((2 * rows, size), f32),
            pltpu.VMEM((FEATURES * 2 * rows, size), f32),
            pltpu.VMEM((all_tiles, 2 * rows), bf16),
            pltpu.VMEM((BOXES, tiles, size), f32),
            pltpu.VMEM((BOXES, tiles, size), f32),
            pltpu.VMEM((BOXES, tiles, size), f32),
            pltpu.VMEM((BOXES, 3, tiles, size), f32),
            pltpu.VMEM((BOXES, 3, tiles, size), f32),
            pltpu.SemaphoreType.DMA((5, BOXES)),
            pltpu.SemaphoreType.DMA((5, BOXES)),
        ],
        compiler_params=pltpu.CompilerParams(collective_id=0, has_side_effects=True),
        name="sph_step",
    )(
        points,
        speeds,
        mass.reshape(tiles, size),
        stiffness.reshape(tiles, size),
        counts.reshape(1, tiles),
        turned,
        turned,
        pair_count,
    )
    new_speeds = speeds + time_step * accel
    new_points = points + time_step * new_speeds
    return (
        new_points.reshape(positions.shape),
        new_speeds.reshape(velocities.shape),
        density.reshape(mass.shape),
    )


def solution(mesh):
    placed = (
        P(None, "gx", "gy", None),
        P(None, "gx", "gy", None),
        P("gx", "gy", None),
        P("gx", "gy", None),
        P("gx", "gy", None),
        P(("gx", "gy"), None),
        P(("gx", "gy")),
    )
    return jax.shard_map(
        functools.partial(body, mesh.shape["gx"], mesh.shape["gy"]),
        mesh=mesh,
        in_specs=placed,
        out_specs=(P(None, "gx", "gy", None), P(None, "gx", "gy", None), P("gx", "gy", None)),
        check_vma=False,
    )
```

```python
import functools
import math

import jax
import jax.numpy as jnp
from jax import lax
from jax.experimental import pallas as pl
from jax.experimental.pallas import tpu as pltpu
from jax.sharding import PartitionSpec as P

kernel_norm = 21.0 / (16.0 * math.pi)
viscosity = 0.1
time_step = 0.02
rest_density = 1.0

MESH = pl.DeviceIdType.MESH
OWN = 2
BOXES = 5
BESIDE = (0, 1, 3, 4)
KDEPTH = 24
FEATURES = 16
UNROLL = 4
FORCE_UNROLL = 8

f32, bf16 = jnp.float32, jnp.bfloat16


def split_in(value, parts):
    pieces = []
    for _ in range(parts):
        piece = value.astype(bf16)
        pieces.append(piece)
        value = value - piece.astype(f32)
    return pieces


def dot_nn(a, b):
    return lax.dot_general(a, b, (((1,), (0,)), ((), ())), preferred_element_type=f32)


def dot_nt(a, b):
    return lax.dot_general(a, b, (((1,), (1,)), ((), ())), preferred_element_type=f32)


def kernel(
    gx, gy, tiles, size, rows,
    pos, vel, mass, stiff, counts, pairs_v, live_s,
    accel_out, density_out,
    pm, vs, side_a, side_b, mass_rows, feats, squares, weights, falls, slope,
    row_density, row_force, picks, table_v, table_s, table_sem,
    dens_part, dens_recv, dens_total, force_part, force_recv, send_sem, recv_sem,
):
    my_x, my_y = lax.axis_index("gx"), lax.axis_index("gy")
    where_to = {
        0: (lax.rem(my_x + gx - 1, gx), my_y),
        1: (my_x, lax.rem(my_y + gy - 1, gy)),
        3: (my_x, lax.rem(my_y + 1, gy)),
        4: (lax.rem(my_x + 1, gx), my_y),
    }
    all_tiles = BOXES * tiles
    plane_step, force_step = all_tiles + 1, 2 * rows + 1

    barrier = pltpu.get_barrier_semaphore()
    for b in BESIDE:
        pl.semaphore_signal(barrier, inc=1, device_id=where_to[b], device_id_type=MESH)

    row_at = lax.broadcasted_iota(jnp.int32, (tiles, tiles), 0)
    column_at = lax.broadcasted_iota(jnp.int32, (tiles, tiles), 1)
    count = jnp.sum(
        jnp.where(row_at == column_at, counts[...].astype(f32), 0.0), axis=1, keepdims=True
    )
    lane = lax.broadcasted_iota(jnp.int32, (tiles, size), 1).astype(f32)
    for c in range(3):
        pm[OWN, c] = 0.5 * (pos[c] - 1.0)
        vs[OWN, c] = vel[c]
    pm[OWN, 3] = jnp.where(lane < count, mass[...], 0.0)
    vs[OWN, 3] = stiff[...]

    pl.semaphore_wait(barrier, len(BESIDE))

    def exchange(stage, source_of, target):
        copies = {}
        for b in BESIDE:
            copies[b] = pltpu.make_async_remote_copy(
                src_ref=source_of(b),
                dst_ref=target.at[4 - b],
                send_sem=send_sem.at[stage, b],
                recv_sem=recv_sem.at[stage, 4 - b],
                device_id=where_to[b],
                device_id_type=MESH,
            )
            copies[b].start()
        return copies

    def arrived(stage, b, target):
        pltpu.make_async_remote_copy(
            src_ref=target.at[b],
            dst_ref=target.at[b],
            send_sem=send_sem.at[stage, b],
            recv_sem=recv_sem.at[stage, b],
            device_id=where_to[b],
            device_id_type=MESH,
        ).wait_recv()

    sent = []
    sent.append(exchange(0, lambda b: pm.at[OWN], pm))
    sent.append(exchange(1, lambda b: vs.at[OWN], vs))

    def at_plane(ref, plane, b):
        return ref.at[pl.ds(plane * plane_step + b * tiles, tiles)]

    def distance_planes(b):
        ones = jnp.ones((tiles, size), f32)
        norm = jnp.zeros((tiles, size), f32)
        planes_a, planes_b = [], []
        for c in range(3):
            h = pm[b, c]
            norm = norm + h * h
            h1, h2, h3 = (p.astype(f32) for p in split_in(h, 3))
            planes_a += [-2.0 * v for v in (h1, h1, h2, h2, h1, h3)]
            planes_b += [h1, h2, h1, h2, h3, h1]
        n_parts = [p.astype(f32) for p in split_in(norm, 3)]
        planes_a += n_parts + [ones] * 3
        planes_b += [ones] * 3 + n_parts
        if b in (0, OWN, 4):
            for k, value in enumerate(planes_a):
                at_plane(side_a, k, b)[...] = value
        if b in (1, OWN, 3):
            for k, value in enumerate(planes_b):
                at_plane(side_b, k, b)[...] = value
        for k, value in enumerate(split_in(pm[b, 3], 2)):
            at_plane(mass_rows, k, b)[...] = value.astype(f32)

    distance_planes(OWN)
    row_density[pl.ds(rows, tiles)] = jnp.zeros((tiles, size), f32)
    for f in range(12):
        row_force[pl.ds(f * force_step + rows, tiles)] = jnp.zeros((tiles, size), f32)

    first = pairs_v[0:1, :]
    second = pairs_v[1:2, :]
    row_index = lax.broadcasted_iota(jnp.int32, (1, rows), 1)
    live = row_index < live_s[0]

    first_tile = (OWN + 2 * (lax.div(first, gy * tiles) - my_x)) * tiles + lax.rem(first, tiles)
    second_tile = (OWN + lax.rem(lax.div(second, tiles), gy) - my_y) * tiles + lax.rem(second, tiles)
    to_first = jnp.where(live, first_tile, -1)
    to_second = jnp.where(live & (first != second), second_tile, -1)
    tile_at = lax.broadcasted_iota(jnp.int32, (all_tiles, rows), 0)
    picks[:, 0:rows] = jnp.where(tile_at == to_first, 1.0, 0.0).astype(bf16)
    picks[:, rows : 2 * rows] = jnp.where(tile_at == to_second, 1.0, 0.0).astype(bf16)
    table_v[0:1] = jnp.clip(first_tile, 0, all_tiles - 1)
    table_v[1:2] = jnp.clip(second_tile, 0, all_tiles - 1)
    table_copy = pltpu.make_async_copy(table_v, table_s, table_sem)
    table_copy.start()

    def own_tiles(r):
        return OWN * tiles + r, OWN * tiles + r

    def listed_tiles(r):
        return table_s[0, r], table_s[1, r]

    def tile_rows(ref, tile, count):
        return ref[pl.ds(tile, count, stride=plane_step), :].astype(bf16)

    def twice(value):
        return jnp.concatenate([value, value], axis=1)

    def side_by_side(value):
        return jnp.concatenate([value[0:size], value[size : 2 * size]], axis=1)

    def distances(u, t1, t2):
        a = tile_rows(side_a, t1, KDEPTH)
        b = tile_rows(side_b, t2, KDEPTH)
        squares[u] = lax.dot_general(a, b, (((0,), (0,)), ((), ())), preferred_element_type=f32)

    def weigh(r, u):
        square = jnp.maximum(squares[u], 1e-13)
        fall = jnp.maximum(1.0 - square * lax.rsqrt(square), 0.0)
        fall2 = fall * fall
        falls[r] = fall
        weight_hi, weight_lo = split_in(fall2 * fall2 * (1.25 - fall), 2)
        weights[u, 0:size] = weight_hi
        weights[u, size : 2 * size] = weight_lo

    def add_up(r, u, t1, t2, cross):
        both = weights[u]
        got = dot_nt(twice(tile_rows(mass_rows, t2, 8)), side_by_side(both))
        row_density[pl.ds(r, 1)] = got[0:1] + got[1:2]
        if cross:
            got = dot_nn(twice(tile_rows(mass_rows, t1, 8)), both)
            row_density[pl.ds(rows + r, 1)] = got[0:1] + got[1:2]

    def density_rows(start, end, tiles_of, cross):
        for u in range(UNROLL):
            distances(u, *tiles_of(start + u))

        def turn(step, carry):
            for u in range(UNROLL):
                r = start + step * UNROLL + u
                before = jnp.maximum(r - UNROLL, start)
                spare = jnp.where(step == 0, 2 * rows + u, before)
                add_up(spare, u, *tiles_of(before), cross)
                weigh(r, u)
                distances(u, *tiles_of(jnp.minimum(r + UNROLL, end - 1)))
            return carry

        lax.fori_loop(0, (end - start) // UNROLL, turn, 0)
        for u in range(UNROLL):
            r = end - UNROLL + u
            add_up(r, u, *tiles_of(r), cross)

    def slopes(start, end):
        def turn(step, carry):
            for u in range(4):
                r = start + step * 4 + u
                fall = falls[r]
                slope_hi, slope_lo = split_in(fall * fall * fall, 2)
                slope[r, 0:size] = slope_hi
                slope[r, size : 2 * size] = slope_lo
            return carry

        lax.fori_loop(0, (end - start) // 4, turn, 0)

    def force_row(r, t1, t2, cross):
        both = slope[r]
        got = dot_nt(twice(tile_rows(feats, t2, 2 * FEATURES)), side_by_side(both))
        row_force[pl.ds(r, FEATURES, stride=force_step), :] = got[0:FEATURES] + got[FEATURES:]
        if cross:
            got = dot_nn(twice(tile_rows(feats, t1, 2 * FEATURES)), both)
            row_force[pl.ds(rows + r, FEATURES, stride=force_step), :] = (
                got[0:FEATURES] + got[FEATURES:]
            )

    def force_rows(start, end, tiles_of, cross):
        def turn(step, carry):
            for u in range(FORCE_UNROLL):
                r = start + step * FORCE_UNROLL + u
                force_row(r, *tiles_of(r), cross)
            return carry

        lax.fori_loop(0, (end - start) // FORCE_UNROLL, turn, 0)

    density_rows(0, tiles, own_tiles, False)
    table_copy.wait()
    for b in BESIDE:
        arrived(0, b, pm)
        distance_planes(b)
    density_rows(tiles, rows, listed_tiles, True)

    chosen = picks[...]
    total = jnp.zeros((all_tiles, size), f32)
    for part in split_in(row_density[0 : 2 * rows], 3):
        total = total + dot_nn(chosen, part)
    dens_part[...] = ((4.0 * kernel_norm) * total).reshape(BOXES, tiles, size)
    sent.append(exchange(2, lambda b: dens_part.at[b], dens_recv))
    slopes(0, rows // 2)
    density = dens_part[OWN]
    for b in BESIDE:
        arrived(2, b, dens_recv)
        density = density + dens_recv[b]
    dens_total[OWN] = density
    density_out[...] = density
    sent.append(exchange(3, lambda b: dens_total.at[OWN], dens_total))

    def pressures(b):
        density = dens_total[b]
        scale = density + 1.0 - jnp.where(pm[b, 3] > 0.0, 1.0, 0.0)
        inverse = 1.0 / scale
        press = vs[b, 3] * (density - rest_density) * inverse * inverse
        return press, inverse

    def force_planes(b):
        press, inverse = pressures(b)
        m = pm[b, 3]
        mp, mq = m * press, m * inverse
        values = [m] + [m * pm[b, c] for c in range(3)]
        values += [mp] + [mp * pm[b, c] for c in range(3)]
        values += [mq] + [mq * vs[b, c] for c in range(3)]
        for k, value in enumerate(values):
            for part, piece in enumerate(split_in(value, 2)):
                at_plane(feats, part * FEATURES + k, b)[...] = piece.astype(f32)

    slopes(rows // 2, rows)
    force_planes(OWN)
    force_rows(0, tiles, own_tiles, False)
    for b in BESIDE:
        arrived(1, b, vs)
        arrived(3, b, dens_total)
        force_planes(b)
    force_rows(tiles, rows, listed_tiles, True)

    sums = []
    for f in range(0, 12, 2):
        pair = [split_in(row_force[pl.ds((f + k) * force_step, 2 * rows)], 2) for k in range(2)]
        total = jnp.zeros((all_tiles, 2 * size), f32)
        for part in range(2):
            total = total + dot_nn(
                chosen, jnp.concatenate([pair[0][part], pair[1][part]], axis=1)
            )
        sums += [total[:, 0:size], total[:, size:]]
    for b in range(BOXES):
        press, inverse = pressures(b)
        s = [v[b * tiles : (b + 1) * tiles] for v in sums]
        for c in range(3):
            h, v = pm[b, c], vs[b, c]
            push = press * (h * s[0] - s[1 + c]) + h * s[4] - s[5 + c]
            drag = inverse * (v * s[8] - s[9 + c])
            force_part[b, c] = (5.0 * kernel_norm) * (2.0 * push - (2.0 * viscosity) * drag)
    sent.append(exchange(4, lambda b: force_part.at[b], force_recv))
    accel = force_part[OWN]
    for b in BESIDE:
        arrived(4, b, force_recv)
        accel = accel + force_recv[b]
    accel_out[...] = accel * jnp.where(pm[OWN, 3] > 0.0, 1.0, 0.0)[None]

    for copies in sent:
        for b in BESIDE:
            copies[b].wait_send()


def body(gx, gy, positions, velocities, mass, stiffness, counts, pairs, pair_count):
    tiles = counts.shape[2]
    size = positions.shape[3] // tiles
    rows = pairs.shape[0]
    all_tiles = BOXES * tiles
    points = positions.reshape(3, tiles, size)
    speeds = velocities.reshape(3, tiles, size)
    turned = pairs.T
    vmem = pl.BlockSpec(memory_space=pltpu.VMEM)
    smem = pl.BlockSpec(memory_space=pltpu.SMEM)
    accel, density = pl.pallas_call(
        functools.partial(kernel, gx, gy, tiles, size, rows),
        out_shape=(
            jax.ShapeDtypeStruct((3, tiles, size), f32),
            jax.ShapeDtypeStruct((tiles, size), f32),
        ),
        in_specs=[vmem] * 6 + [smem],
        out_specs=(vmem, vmem),
        scratch_shapes=[
            pltpu.VMEM((BOXES, 4, tiles, size), f32),
            pltpu.VMEM((BOXES, 4, tiles, size), f32),
            pltpu.VMEM((KDEPTH * (all_tiles + 1), size), f32),
            pltpu.VMEM((KDEPTH * (all_tiles + 1), size), f32),
            pltpu.VMEM((8 * (all_tiles + 1), size), f32),
            pltpu.VMEM((2 * FEATURES * (all_tiles + 1), size), f32),
            pltpu.VMEM((UNROLL, size, size), f32),
            pltpu.VMEM((UNROLL, 2 * size, size), bf16),
            pltpu.VMEM((rows, size, size), f32),
            pltpu.VMEM((rows, 2 * size, size), bf16),
            pltpu.VMEM((3 * rows + 8, size), f32),
            pltpu.VMEM((FEATURES * (2 * rows + 1), size), f32),
            pltpu.VMEM((all_tiles, 2 * rows), bf16),
            pltpu.VMEM((2, rows), jnp.int32),
            pltpu.SMEM((2, rows), jnp.int32),
            pltpu.SemaphoreType.DMA,
            pltpu.VMEM((BOXES, tiles, size), f32),
            pltpu.VMEM((BOXES, tiles, size), f32),
            pltpu.VMEM((BOXES, tiles, size), f32),
            pltpu.VMEM((BOXES, 3, tiles, size), f32),
            pltpu.VMEM((BOXES, 3, tiles, size), f32),
            pltpu.SemaphoreType.DMA((5, BOXES)),
            pltpu.SemaphoreType.DMA((5, BOXES)),
        ],
        compiler_params=pltpu.CompilerParams(collective_id=0, has_side_effects=True),
        name="sph_step",
    )(
        points,
        speeds,
        mass.reshape(tiles, size),
        stiffness.reshape(tiles, size),
        counts.reshape(1, tiles),
        turned,
        pair_count,
    )
    new_speeds = speeds + time_step * accel
    new_points = points + time_step * new_speeds
    return (
        new_points.reshape(positions.shape),
        new_speeds.reshape(velocities.shape),
        density.reshape(mass.shape),
    )


def solution(mesh):
    placed = (
        P(None, "gx", "gy", None),
        P(None, "gx", "gy", None),
        P("gx", "gy", None),
        P("gx", "gy", None),
        P("gx", "gy", None),
        P(("gx", "gy"), None),
        P(("gx", "gy")),
    )
    return jax.shard_map(
        functools.partial(body, mesh.shape["gx"], mesh.shape["gy"]),
        mesh=mesh,
        in_specs=placed,
        out_specs=(P(None, "gx", "gy", None), P(None, "gx", "gy", None), P("gx", "gy", None)),
        check_vma=False,
    )
```

```python
import functools
import math

import jax
import jax.numpy as jnp
from jax import lax
from jax.experimental import pallas as pl
from jax.experimental.pallas import tpu as pltpu
from jax.sharding import PartitionSpec as P

kernel_norm = 21.0 / (16.0 * math.pi)
viscosity = 0.1
time_step = 0.02
rest_density = 1.0

MESH = pl.DeviceIdType.MESH
OWN = 2
BOXES = 5
BESIDE = (0, 1, 3, 4)
KDEPTH = 24
FEATURES = 16
UNROLL = 8
FORCE_UNROLL = 8

f32, bf16 = jnp.float32, jnp.bfloat16


def split_in(value, parts):
    pieces = []
    for _ in range(parts):
        piece = value.astype(bf16)
        pieces.append(piece)
        value = value - piece.astype(f32)
    return pieces


def dot_nn(a, b):
    return lax.dot_general(a, b, (((1,), (0,)), ((), ())), preferred_element_type=f32)


def dot_nt(a, b):
    return lax.dot_general(a, b, (((1,), (1,)), ((), ())), preferred_element_type=f32)


def kernel(
    gx, gy, tiles, size, rows,
    pos_h, vel_h, mass_h, stiff_h, counts_h, pairs_h, live_s,
    points_out, speeds_out, density_out,
    pos, mass, counts, pairs_v, in_sem,
    pm, vs, side_a, side_b, mass_rows, feats, squares, weights, falls, slope,
    row_density, row_force, picks, table_v, table_s, table_sem,
    dens_part, dens_recv, dens_total, force_part, force_recv, send_sem, recv_sem,
):
    my_x, my_y = lax.axis_index("gx"), lax.axis_index("gy")
    where_to = {
        0: (my_x - 1, my_y),
        1: (my_x, my_y - 1),
        3: (my_x, my_y + 1),
        4: (my_x + 1, my_y),
    }
    there = {0: my_x > 0, 1: my_y > 0, 3: my_y < gy - 1, 4: my_x < gx - 1}
    all_tiles = BOXES * tiles
    plane_step, force_step = all_tiles + 1, 2 * rows + 1

    barrier = pltpu.get_barrier_semaphore()
    for b in BESIDE:

        @pl.when(there[b])
        def _(b=b):
            pl.semaphore_signal(barrier, inc=1, device_id=where_to[b], device_id_type=MESH)


    inputs = (
        (pos_h, pos),
        (mass_h, mass),
        (counts_h, counts),
        (pairs_h, pairs_v),
        (vel_h, vs.at[OWN, 0:3]),
        (stiff_h, vs.at[OWN, 3]),
    )
    loads = [pltpu.make_async_copy(a, b, in_sem.at[k]) for k, (a, b) in enumerate(inputs)]
    for load in loads:
        load.start()

    for load in loads[0:3]:
        load.wait()
    row_at = lax.broadcasted_iota(jnp.int32, (tiles, tiles), 0)
    column_at = lax.broadcasted_iota(jnp.int32, (tiles, tiles), 1)
    count = jnp.sum(
        jnp.where(row_at == column_at, counts[...].astype(f32), 0.0), axis=1, keepdims=True
    )
    lane = lax.broadcasted_iota(jnp.int32, (tiles, size), 1).astype(f32)
    for c in range(3):
        pm[OWN, c] = 0.5 * (pos[c] - 1.0)
    pm[OWN, 3] = jnp.where(lane < count, mass[...], 0.0)

    pl.semaphore_wait(barrier, sum(there[b].astype(jnp.int32) for b in BESIDE))

    def copy_to(stage, b, source, target):
        return pltpu.make_async_remote_copy(
            src_ref=source,
            dst_ref=target.at[4 - b],
            send_sem=send_sem.at[stage, b],
            recv_sem=recv_sem.at[stage, 4 - b],
            device_id=where_to[b],
            device_id_type=MESH,
        )

    def exchange(stage, source_of, target):
        for b in BESIDE:

            @pl.when(there[b])
            def _(b=b):
                copy_to(stage, b, source_of(b), target).start()

        return stage, source_of, target

    def arrived(stage, b, target):
        @pl.when(there[b])
        def _():
            pltpu.make_async_remote_copy(
                src_ref=target.at[b],
                dst_ref=target.at[b],
                send_sem=send_sem.at[stage, b],
                recv_sem=recv_sem.at[stage, b],
                device_id=where_to[b],
                device_id_type=MESH,
            ).wait_recv()

    sent = []
    sent.append(exchange(0, lambda b: pm.at[OWN], pm))

    def at_plane(ref, plane, b):
        return ref.at[pl.ds(plane * plane_step + b * tiles, tiles)]

    def distance_planes(b):
        ones = jnp.ones((tiles, size), f32)
        norm = jnp.zeros((tiles, size), f32)
        planes_a, planes_b = [], []
        for c in range(3):
            h = pm[b, c]
            norm = norm + h * h
            h1, h2, h3 = (p.astype(f32) for p in split_in(h, 3))
            planes_a += [-2.0 * v for v in (h1, h1, h2, h2, h1, h3)]
            planes_b += [h1, h2, h1, h2, h3, h1]
        n_parts = [p.astype(f32) for p in split_in(norm, 3)]
        planes_a += n_parts + [ones] * 3
        planes_b += [ones] * 3 + n_parts
        if b in (0, OWN, 4):
            for k, value in enumerate(planes_a):
                at_plane(side_a, k, b)[...] = value
        if b in (1, OWN, 3):
            for k, value in enumerate(planes_b):
                at_plane(side_b, k, b)[...] = value
        for k, value in enumerate(split_in(pm[b, 3], 2)):
            at_plane(mass_rows, k, b)[...] = value.astype(f32)

    distance_planes(OWN)
    row_density[pl.ds(rows, tiles)] = jnp.zeros((tiles, size), f32)
    for f in range(12):
        row_force[pl.ds(f * force_step + rows, tiles)] = jnp.zeros((tiles, size), f32)

    loads[3].wait()
    first = pairs_v[0:1, :]
    second = pairs_v[1:2, :]
    row_index = lax.broadcasted_iota(jnp.int32, (1, rows), 1)
    live = row_index < live_s[0]

    first_tile = (OWN + 2 * (lax.div(first, gy * tiles) - my_x)) * tiles + lax.rem(first, tiles)
    second_tile = (OWN + lax.rem(lax.div(second, tiles), gy) - my_y) * tiles + lax.rem(second, tiles)
    to_first = jnp.where(live, first_tile, -1)
    to_second = jnp.where(live & (first != second), second_tile, -1)
    tile_at = lax.broadcasted_iota(jnp.int32, (all_tiles, rows), 0)
    picks[:, 0:rows] = jnp.where(tile_at == to_first, 1.0, 0.0).astype(bf16)
    picks[:, rows : 2 * rows] = jnp.where(tile_at == to_second, 1.0, 0.0).astype(bf16)
    table_v[0:1] = jnp.clip(first_tile, 0, all_tiles - 1)
    table_v[1:2] = jnp.clip(second_tile, 0, all_tiles - 1)
    table_copy = pltpu.make_async_copy(table_v, table_s, table_sem)
    table_copy.start()

    def own_tiles(r):
        return OWN * tiles + r, OWN * tiles + r

    def listed_tiles(r):
        return table_s[0, r], table_s[1, r]

    def tile_rows(ref, tile, count):
        return ref[pl.ds(tile, count, stride=plane_step), :].astype(bf16)

    def twice(value):
        return jnp.concatenate([value, value], axis=1)

    def side_by_side(value):
        return jnp.concatenate([value[0:size], value[size : 2 * size]], axis=1)

    def distances(u, t1, t2):
        a = tile_rows(side_a, t1, KDEPTH)
        b = tile_rows(side_b, t2, KDEPTH)
        squares[u] = lax.dot_general(a, b, (((0,), (0,)), ((), ())), preferred_element_type=f32)

    def weigh(r, u):
        square = jnp.maximum(squares[u], 1e-13)
        fall = jnp.maximum(1.0 - square * lax.rsqrt(square), 0.0)
        fall2 = fall * fall
        falls[r] = fall
        weight_hi, weight_lo = split_in(fall2 * fall2 * (1.25 - fall), 2)
        weights[u, 0:size] = weight_hi
        weights[u, size : 2 * size] = weight_lo

    def add_up(r, u, t1, t2, cross):
        both = weights[u]
        got = dot_nt(twice(tile_rows(mass_rows, t2, 8)), side_by_side(both))
        row_density[pl.ds(r, 1)] = got[0:1] + got[1:2]
        if cross:
            got = dot_nn(twice(tile_rows(mass_rows, t1, 8)), both)
            row_density[pl.ds(rows + r, 1)] = got[0:1] + got[1:2]

    def density_rows(start, end, tiles_of, cross):
        for u in range(UNROLL):
            distances(u, *tiles_of(start + u))

        def turn(step, carry):
            for u in range(UNROLL):
                r = start + step * UNROLL + u
                before = jnp.maximum(r - UNROLL, start)
                spare = jnp.where(step == 0, 2 * rows + u, before)
                add_up(spare, u, *tiles_of(before), cross)
                weigh(r, u)
                distances(u, *tiles_of(jnp.minimum(r + UNROLL, end - 1)))
            return carry

        lax.fori_loop(0, (end - start) // UNROLL, turn, 0)
        for u in range(UNROLL):
            r = end - UNROLL + u
            add_up(r, u, *tiles_of(r), cross)

    def slopes(start, end):
        def turn(step, carry):
            for u in range(4):
                r = start + step * 4 + u
                fall = falls[r]
                slope_hi, slope_lo = split_in(fall * fall * fall, 2)
                slope[r, 0:size] = slope_hi
                slope[r, size : 2 * size] = slope_lo
            return carry

        lax.fori_loop(0, (end - start) // 4, turn, 0)

    def force_row(r, t1, t2, cross):
        both = slope[r]
        got = dot_nt(twice(tile_rows(feats, t2, 2 * FEATURES)), side_by_side(both))
        row_force[pl.ds(r, FEATURES, stride=force_step), :] = got[0:FEATURES] + got[FEATURES:]
        if cross:
            got = dot_nn(twice(tile_rows(feats, t1, 2 * FEATURES)), both)
            row_force[pl.ds(rows + r, FEATURES, stride=force_step), :] = (
                got[0:FEATURES] + got[FEATURES:]
            )

    def force_rows(start, end, tiles_of, cross):
        def turn(step, carry):
            for u in range(FORCE_UNROLL):
                r = start + step * FORCE_UNROLL + u
                force_row(r, *tiles_of(r), cross)
            return carry

        lax.fori_loop(0, (end - start) // FORCE_UNROLL, turn, 0)

    density_rows(0, tiles, own_tiles, False)
    table_copy.wait()
    for b in BESIDE:
        arrived(0, b, pm)
        distance_planes(b)
    for load in loads[4:6]:
        load.wait()
    sent.append(exchange(1, lambda b: vs.at[OWN], vs))
    density_rows(tiles, rows, listed_tiles, True)

    chosen = picks[...]
    total = jnp.zeros((all_tiles, size), f32)
    for part in split_in(row_density[0 : 2 * rows], 3):
        total = total + dot_nn(chosen, part)
    dens_part[...] = ((4.0 * kernel_norm) * total).reshape(BOXES, tiles, size)
    sent.append(exchange(2, lambda b: dens_part.at[b], dens_recv))
    slopes(0, rows // 2)
    density = dens_part[OWN]
    for b in BESIDE:
        arrived(2, b, dens_recv)
        density = density + jnp.where(there[b], dens_recv[b], 0.0)
    dens_total[OWN] = density
    density_out[...] = density
    sent.append(exchange(3, lambda b: dens_total.at[OWN], dens_total))

    def pressures(b):
        density = dens_total[b]
        scale = density + 1.0 - jnp.where(pm[b, 3] > 0.0, 1.0, 0.0)
        inverse = 1.0 / scale
        press = vs[b, 3] * (density - rest_density) * inverse * inverse
        return press, inverse

    def force_planes(b):
        press, inverse = pressures(b)
        m = pm[b, 3]
        mp, mq = m * press, m * inverse
        values = [m] + [m * pm[b, c] for c in range(3)]
        values += [mp] + [mp * pm[b, c] for c in range(3)]
        values += [mq] + [mq * vs[b, c] for c in range(3)]
        for k, value in enumerate(values):
            for part, piece in enumerate(split_in(value, 2)):
                at_plane(feats, part * FEATURES + k, b)[...] = piece.astype(f32)

    slopes(rows // 2, rows)
    force_planes(OWN)
    force_rows(0, tiles, own_tiles, False)
    for b in BESIDE:
        arrived(1, b, vs)
        arrived(3, b, dens_total)
        force_planes(b)
    force_rows(tiles, rows, listed_tiles, True)

    sums = []
    for f in range(0, 12, 2):
        pair = [split_in(row_force[pl.ds((f + k) * force_step, 2 * rows)], 2) for k in range(2)]
        total = jnp.zeros((all_tiles, 2 * size), f32)
        for part in range(2):
            total = total + dot_nn(
                chosen, jnp.concatenate([pair[0][part], pair[1][part]], axis=1)
            )
        sums += [total[:, 0:size], total[:, size:]]
    for b in range(BOXES):
        press, inverse = pressures(b)
        s = [v[b * tiles : (b + 1) * tiles] for v in sums]
        for c in range(3):
            h, v = pm[b, c], vs[b, c]
            push = press * (h * s[0] - s[1 + c]) + h * s[4] - s[5 + c]
            drag = inverse * (v * s[8] - s[9 + c])
            force_part[b, c] = (5.0 * kernel_norm) * (2.0 * push - (2.0 * viscosity) * drag)
    sent.append(exchange(4, lambda b: force_part.at[b], force_recv))
    accel = force_part[OWN]
    for b in BESIDE:
        arrived(4, b, force_recv)
        accel = accel + jnp.where(there[b], force_recv[b], 0.0)
    accel = accel * jnp.where(pm[OWN, 3] > 0.0, 1.0, 0.0)[None]
    new_speeds = vs[OWN, 0:3] + time_step * accel
    speeds_out[...] = new_speeds
    points_out[...] = pos[...] + time_step * new_speeds

    for stage, source_of, target in sent:
        for b in BESIDE:

            @pl.when(there[b])
            def _(b=b):
                copy_to(stage, b, source_of(b), target).wait_send()


def store_kernel(points, speeds, density, points_out, speeds_out, density_out, sem):
    pairs = ((points, points_out), (speeds, speeds_out), (density, density_out))
    stores = [pltpu.make_async_copy(a, b, sem.at[k]) for k, (a, b) in enumerate(pairs)]
    for store in stores:
        store.start()
    for store in stores:
        store.wait()


def body(gx, gy, positions, velocities, mass, stiffness, counts, pairs, pair_count):
    tiles = counts.shape[2]
    size = positions.shape[3] // tiles
    rows = pairs.shape[0]
    all_tiles = BOXES * tiles
    points = positions.reshape(3, tiles, size)
    speeds = velocities.reshape(3, tiles, size)
    turned = pairs.T
    vmem = pl.BlockSpec(memory_space=pltpu.VMEM)
    hbm = pl.BlockSpec(memory_space=pltpu.HBM)
    shapes = (
        jax.ShapeDtypeStruct((3, tiles, size), f32),
        jax.ShapeDtypeStruct((3, tiles, size), f32),
        jax.ShapeDtypeStruct((tiles, size), f32),
    )
    results = pl.pallas_call(
        functools.partial(kernel, gx, gy, tiles, size, rows),
        out_shape=shapes,
        in_specs=[hbm] * 6 + [pl.BlockSpec(memory_space=pltpu.SMEM)],
        out_specs=(vmem,) * 3,
        scratch_shapes=[
            pltpu.VMEM((3, tiles, size), f32),
            pltpu.VMEM((tiles, size), f32),
            pltpu.VMEM((1, tiles), jnp.int32),
            pltpu.VMEM((2, rows), jnp.int32),
            pltpu.SemaphoreType.DMA((6,)),
            pltpu.VMEM((BOXES, 4, tiles, size), f32),
            pltpu.VMEM((BOXES, 4, tiles, size), f32),
            pltpu.VMEM((KDEPTH * (all_tiles + 1), size), f32),
            pltpu.VMEM((KDEPTH * (all_tiles + 1), size), f32),
            pltpu.VMEM((8 * (all_tiles + 1), size), f32),
            pltpu.VMEM((2 * FEATURES * (all_tiles + 1), size), f32),
            pltpu.VMEM((UNROLL, size, size), f32),
            pltpu.VMEM((UNROLL, 2 * size, size), bf16),
            pltpu.VMEM((rows, size, size), f32),
            pltpu.VMEM((rows, 2 * size, size), bf16),
            pltpu.VMEM((3 * rows + 8, size), f32),
            pltpu.VMEM((FEATURES * (2 * rows + 1), size), f32),
            pltpu.VMEM((all_tiles, 2 * rows), bf16),
            pltpu.VMEM((2, rows), jnp.int32),
            pltpu.SMEM((2, rows), jnp.int32),
            pltpu.SemaphoreType.DMA,
            pltpu.VMEM((BOXES, tiles, size), f32),
            pltpu.VMEM((BOXES, tiles, size), f32),
            pltpu.VMEM((BOXES, tiles, size), f32),
            pltpu.VMEM((BOXES, 3, tiles, size), f32),
            pltpu.VMEM((BOXES, 3, tiles, size), f32),
            pltpu.SemaphoreType.DMA((5, BOXES)),
            pltpu.SemaphoreType.DMA((5, BOXES)),
        ],
        compiler_params=pltpu.CompilerParams(collective_id=0, has_side_effects=True, vmem_limit_bytes=40 << 20),
        name="sph_step",
    )(
        *(
            pltpu.with_memory_space_constraint(value, pltpu.HBM)
            for value in (
                points,
                speeds,
                mass.reshape(tiles, size),
                stiffness.reshape(tiles, size),
                counts.reshape(1, tiles),
                turned,
            )
        ),
        pair_count,
    )
    new_points, new_speeds, density = pl.pallas_call(
        store_kernel,
        out_shape=shapes,
        in_specs=[vmem] * 3,
        out_specs=(hbm,) * 3,
        scratch_shapes=[pltpu.SemaphoreType.DMA((3,))],
        compiler_params=pltpu.CompilerParams(vmem_limit_bytes=1 << 20),
        name="sph_store",
    )(*results)
    return (
        new_points.reshape(positions.shape),
        new_speeds.reshape(velocities.shape),
        density.reshape(mass.shape),
    )


def solution(mesh):
    placed = (
        P(None, "gx", "gy", None),
        P(None, "gx", "gy", None),
        P("gx", "gy", None),
        P("gx", "gy", None),
        P("gx", "gy", None),
        P(("gx", "gy"), None),
        P(("gx", "gy")),
    )
    return jax.shard_map(
        functools.partial(body, mesh.shape["gx"], mesh.shape["gy"]),
        mesh=mesh,
        in_specs=placed,
        out_specs=(P(None, "gx", "gy", None), P(None, "gx", "gy", None), P("gx", "gy", None)),
        check_vma=False,
    )
```

```python
import functools
import math

import jax
import jax.numpy as jnp
from jax import lax
from jax.experimental import pallas as pl
from jax.experimental.pallas import tpu as pltpu
from jax.sharding import PartitionSpec as P

kernel_norm = 21.0 / (16.0 * math.pi)
viscosity = 0.1
time_step = 0.02
rest_density = 1.0

MESH = pl.DeviceIdType.MESH
OWN = 2
BOXES = 5
BESIDE = (0, 1, 3, 4)
KDEPTH = 24
FEATURES = 16
UNROLL = 16
FORCE_UNROLL = 32

f32, bf16 = jnp.float32, jnp.bfloat16


def split_in(value, parts):
    pieces = []
    for _ in range(parts):
        piece = value.astype(bf16)
        pieces.append(piece)
        value = value - piece.astype(f32)
    return pieces


def dot_nn(a, b):
    return lax.dot_general(a, b, (((1,), (0,)), ((), ())), preferred_element_type=f32)


def dot_nt(a, b):
    return lax.dot_general(a, b, (((1,), (1,)), ((), ())), preferred_element_type=f32)


def kernel(
    gx, gy, tiles, size, rows,
    pos_h, vel_h, mass_h, stiff_h, counts_h, pairs_h, live_s,
    points_out, speeds_out, density_out,
    pos, mass, counts, pairs_v, in_sem,
    pm, vs, side_a, side_b, mass_rows, feats, squares, weights, falls, slope,
    row_density, row_force, picks, table_v, table_s, table_sem,
    dens_part, dens_recv, dens_total, force_part, force_recv, send_sem, recv_sem,
):
    my_x, my_y = lax.axis_index("gx"), lax.axis_index("gy")
    where_to = {
        0: (my_x - 1, my_y),
        1: (my_x, my_y - 1),
        3: (my_x, my_y + 1),
        4: (my_x + 1, my_y),
    }
    there = {0: my_x > 0, 1: my_y > 0, 3: my_y < gy - 1, 4: my_x < gx - 1}
    all_tiles = BOXES * tiles
    plane_step, force_step = all_tiles + 1, 2 * rows + 1

    barrier = pltpu.get_barrier_semaphore()
    for b in BESIDE:

        @pl.when(there[b])
        def _(b=b):
            pl.semaphore_signal(barrier, inc=1, device_id=where_to[b], device_id_type=MESH)


    inputs = (
        (pos_h, pos),
        (mass_h, mass),
        (counts_h, counts),
        (pairs_h, pairs_v),
        (vel_h, vs.at[OWN, 0:3]),
        (stiff_h, vs.at[OWN, 3]),
    )
    loads = [pltpu.make_async_copy(a, b, in_sem.at[k]) for k, (a, b) in enumerate(inputs)]
    for load in loads:
        load.start()

    for load in loads[0:3]:
        load.wait()
    row_at = lax.broadcasted_iota(jnp.int32, (tiles, tiles), 0)
    column_at = lax.broadcasted_iota(jnp.int32, (tiles, tiles), 1)
    count = jnp.sum(
        jnp.where(row_at == column_at, counts[...].astype(f32), 0.0), axis=1, keepdims=True
    )
    lane = lax.broadcasted_iota(jnp.int32, (tiles, size), 1).astype(f32)
    for c in range(3):
        pm[OWN, c] = 0.5 * (pos[c] - 1.0)
    pm[OWN, 3] = jnp.where(lane < count, mass[...], 0.0)

    pl.semaphore_wait(barrier, sum(there[b].astype(jnp.int32) for b in BESIDE))

    def copy_to(stage, b, source, target):
        return pltpu.make_async_remote_copy(
            src_ref=source,
            dst_ref=target.at[4 - b],
            send_sem=send_sem.at[stage, b],
            recv_sem=recv_sem.at[stage, 4 - b],
            device_id=where_to[b],
            device_id_type=MESH,
        )

    def send_to(stage, b, source, target):
        @pl.when(there[b])
        def _():
            copy_to(stage, b, source, target).start()

    def exchange(stage, source_of, target):
        for b in BESIDE:
            send_to(stage, b, source_of(b), target)
        return stage, source_of, target

    def arrived(stage, b, target):
        @pl.when(there[b])
        def _():
            pltpu.make_async_remote_copy(
                src_ref=target.at[b],
                dst_ref=target.at[b],
                send_sem=send_sem.at[stage, b],
                recv_sem=recv_sem.at[stage, b],
                device_id=where_to[b],
                device_id_type=MESH,
            ).wait_recv()

    sent = []
    sent.append(exchange(0, lambda b: pm.at[OWN], pm))

    def at_plane(ref, plane, b):
        return ref.at[pl.ds(plane * plane_step + b * tiles, tiles)]

    def distance_planes(b):
        ones = jnp.ones((tiles, size), f32)
        norm = jnp.zeros((tiles, size), f32)
        planes_a, planes_b = [], []
        for c in range(3):
            h = pm[b, c]
            norm = norm + h * h
            h1, h2, h3 = (p.astype(f32) for p in split_in(h, 3))
            planes_a += [-2.0 * v for v in (h1, h1, h2, h2, h1, h3)]
            planes_b += [h1, h2, h1, h2, h3, h1]
        n_parts = [p.astype(f32) for p in split_in(norm, 3)]
        planes_a += n_parts + [ones] * 3
        planes_b += [ones] * 3 + n_parts
        if b in (0, OWN, 4):
            for k, value in enumerate(planes_a):
                at_plane(side_a, k, b)[...] = value
        if b in (1, OWN, 3):
            for k, value in enumerate(planes_b):
                at_plane(side_b, k, b)[...] = value
        for k, value in enumerate(split_in(pm[b, 3], 2)):
            at_plane(mass_rows, k, b)[...] = value.astype(f32)

    distance_planes(OWN)
    row_density[pl.ds(rows, tiles)] = jnp.zeros((tiles, size), f32)
    for f in range(12):
        row_force[pl.ds(f * force_step + rows, tiles)] = jnp.zeros((tiles, size), f32)

    loads[3].wait()
    first = pairs_v[0:1, :]
    second = pairs_v[1:2, :]
    row_index = lax.broadcasted_iota(jnp.int32, (1, rows), 1)
    live = row_index < live_s[0]

    first_tile = (OWN + 2 * (lax.div(first, gy * tiles) - my_x)) * tiles + lax.rem(first, tiles)
    second_tile = (OWN + lax.rem(lax.div(second, tiles), gy) - my_y) * tiles + lax.rem(second, tiles)
    to_first = jnp.where(live, first_tile, -1)
    to_second = jnp.where(live & (first != second), second_tile, -1)
    tile_at = lax.broadcasted_iota(jnp.int32, (all_tiles, rows), 0)
    picks[:, 0:rows] = jnp.where(tile_at == to_first, 1.0, 0.0).astype(bf16)
    picks[:, rows : 2 * rows] = jnp.where(tile_at == to_second, 1.0, 0.0).astype(bf16)
    table_v[0:1] = jnp.clip(first_tile, 0, all_tiles - 1)
    table_v[1:2] = jnp.clip(second_tile, 0, all_tiles - 1)
    table_copy = pltpu.make_async_copy(table_v, table_s, table_sem)
    table_copy.start()

    def own_tiles(r):
        return OWN * tiles + r, OWN * tiles + r

    def listed_tiles(r):
        return table_s[0, r], table_s[1, r]

    def tile_rows(ref, tile, count):
        return ref[pl.ds(tile, count, stride=plane_step), :].astype(bf16)

    def twice(value):
        return jnp.concatenate([value, value], axis=1)

    def side_by_side(value):
        return jnp.concatenate([value[0:size], value[size : 2 * size]], axis=1)

    def distances(u, t1, t2):
        a = tile_rows(side_a, t1, KDEPTH)
        b = tile_rows(side_b, t2, KDEPTH)
        squares[u] = lax.dot_general(a, b, (((0,), (0,)), ((), ())), preferred_element_type=f32)

    def weigh(r, u):
        square = jnp.maximum(squares[u], 1e-13)
        fall = jnp.maximum(1.0 - square * lax.rsqrt(square), 0.0)
        fall2 = fall * fall
        falls[r] = fall
        weight_hi, weight_lo = split_in(fall2 * fall2 * (1.25 - fall), 2)
        weights[u, 0:size] = weight_hi
        weights[u, size : 2 * size] = weight_lo

    def add_up(r, u, t1, t2, cross):
        both = weights[u]
        got = dot_nt(twice(tile_rows(mass_rows, t2, 8)), side_by_side(both))
        row_density[pl.ds(r, 1)] = got[0:1] + got[1:2]
        if cross:
            got = dot_nn(twice(tile_rows(mass_rows, t1, 8)), both)
            row_density[pl.ds(rows + r, 1)] = got[0:1] + got[1:2]

    def density_rows(start, end, tiles_of, cross):
        for u in range(UNROLL):
            distances(u, *tiles_of(start + u))

        def turn(step, carry):
            for u in range(UNROLL):
                r = start + step * UNROLL + u
                before = jnp.maximum(r - UNROLL, start)
                spare = jnp.where(step == 0, 2 * rows + u, before)
                add_up(spare, u, *tiles_of(before), cross)
                weigh(r, u)
                distances(u, *tiles_of(jnp.minimum(r + UNROLL, end - 1)))
            return carry

        lax.fori_loop(0, (end - start) // UNROLL, turn, 0)
        for u in range(UNROLL):
            r = end - UNROLL + u
            add_up(r, u, *tiles_of(r), cross)

    def slopes(start, end):
        def turn(step, carry):
            for u in range(4):
                r = start + step * 4 + u
                fall = falls[r]
                slope_hi, slope_lo = split_in(fall * fall * fall, 2)
                slope[r, 0:size] = slope_hi
                slope[r, size : 2 * size] = slope_lo
            return carry

        lax.fori_loop(0, (end - start) // 4, turn, 0)

    def force_row(r, t1, t2, cross):
        both = slope[r]
        got = dot_nt(twice(tile_rows(feats, t2, 2 * FEATURES)), side_by_side(both))
        row_force[pl.ds(r, FEATURES, stride=force_step), :] = got[0:FEATURES] + got[FEATURES:]
        if cross:
            got = dot_nn(twice(tile_rows(feats, t1, 2 * FEATURES)), both)
            row_force[pl.ds(rows + r, FEATURES, stride=force_step), :] = (
                got[0:FEATURES] + got[FEATURES:]
            )

    def force_rows(start, end, tiles_of, cross):
        def turn(step, carry):
            for u in range(FORCE_UNROLL):
                r = start + step * FORCE_UNROLL + u
                force_row(r, *tiles_of(r), cross)
            return carry

        lax.fori_loop(0, (end - start) // FORCE_UNROLL, turn, 0)

    density_rows(0, tiles, own_tiles, False)
    table_copy.wait()
    for b in BESIDE:
        arrived(0, b, pm)
        distance_planes(b)
    for load in loads[4:6]:
        load.wait()
    sent.append(exchange(1, lambda b: vs.at[OWN], vs))
    density_rows(tiles, rows, listed_tiles, True)

    chosen = picks[...]
    total = jnp.zeros((all_tiles, size), f32)
    for part in split_in(row_density[0 : 2 * rows], 3):
        total = total + dot_nn(chosen, part)
    dens_part[...] = ((4.0 * kernel_norm) * total).reshape(BOXES, tiles, size)
    sent.append(exchange(2, lambda b: dens_part.at[b], dens_recv))
    slopes(0, rows // 2)
    density = dens_part[OWN]
    for b in BESIDE:
        arrived(2, b, dens_recv)
        density = density + jnp.where(there[b], dens_recv[b], 0.0)
    dens_total[OWN] = density
    density_out[...] = density
    sent.append(exchange(3, lambda b: dens_total.at[OWN], dens_total))

    def pressures(b):
        density = dens_total[b]
        scale = density + 1.0 - jnp.where(pm[b, 3] > 0.0, 1.0, 0.0)
        inverse = 1.0 / scale
        press = vs[b, 3] * (density - rest_density) * inverse * inverse
        return press, inverse

    def force_planes(b):
        press, inverse = pressures(b)
        m = pm[b, 3]
        mp, mq = m * press, m * inverse
        values = [m] + [m * pm[b, c] for c in range(3)]
        values += [mp] + [mp * pm[b, c] for c in range(3)]
        values += [mq] + [mq * vs[b, c] for c in range(3)]
        for k, value in enumerate(values):
            for part, piece in enumerate(split_in(value, 2)):
                at_plane(feats, part * FEATURES + k, b)[...] = piece.astype(f32)

    slopes(rows // 2, rows)
    force_planes(OWN)
    force_rows(0, tiles, own_tiles, False)
    for b in BESIDE:
        arrived(1, b, vs)
        arrived(3, b, dens_total)
        force_planes(b)
    force_rows(tiles, rows, listed_tiles, True)

    sums = []
    for f in range(0, 12, 2):
        pair = [split_in(row_force[pl.ds((f + k) * force_step, 2 * rows)], 2) for k in range(2)]
        total = jnp.zeros((all_tiles, 2 * size), f32)
        for part in range(2):
            total = total + dot_nn(
                chosen, jnp.concatenate([pair[0][part], pair[1][part]], axis=1)
            )
        sums += [total[:, 0:size], total[:, size:]]
    sent.append((4, lambda b: force_part.at[b], force_recv))
    for b in BESIDE + (OWN,):
        press, inverse = pressures(b)
        s = [v[b * tiles : (b + 1) * tiles] for v in sums]
        for c in range(3):
            h, v = pm[b, c], vs[b, c]
            push = press * (h * s[0] - s[1 + c]) + h * s[4] - s[5 + c]
            drag = inverse * (v * s[8] - s[9 + c])
            force_part[b, c] = (5.0 * kernel_norm) * (2.0 * push - (2.0 * viscosity) * drag)
        if b != OWN:
            send_to(4, b, force_part.at[b], force_recv)
    accel = force_part[OWN]
    for b in BESIDE:
        arrived(4, b, force_recv)
        accel = accel + jnp.where(there[b], force_recv[b], 0.0)
    accel = accel * jnp.where(pm[OWN, 3] > 0.0, 1.0, 0.0)[None]
    new_speeds = vs[OWN, 0:3] + time_step * accel
    speeds_out[...] = new_speeds
    points_out[...] = pos[...] + time_step * new_speeds

    for stage, source_of, target in sent:
        for b in BESIDE:

            @pl.when(there[b])
            def _(b=b):
                copy_to(stage, b, source_of(b), target).wait_send()


def store_kernel(points, speeds, density, points_out, speeds_out, density_out, sem):
    pairs = ((points, points_out), (speeds, speeds_out), (density, density_out))
    stores = [pltpu.make_async_copy(a, b, sem.at[k]) for k, (a, b) in enumerate(pairs)]
    for store in stores:
        store.start()
    for store in stores:
        store.wait()


def body(gx, gy, positions, velocities, mass, stiffness, counts, pairs, pair_count):
    tiles = counts.shape[2]
    size = positions.shape[3] // tiles
    rows = pairs.shape[0]
    all_tiles = BOXES * tiles
    points = positions.reshape(3, tiles, size)
    speeds = velocities.reshape(3, tiles, size)
    turned = pairs.T
    vmem = pl.BlockSpec(memory_space=pltpu.VMEM)
    hbm = pl.BlockSpec(memory_space=pltpu.HBM)
    shapes = (
        jax.ShapeDtypeStruct((3, tiles, size), f32),
        jax.ShapeDtypeStruct((3, tiles, size), f32),
        jax.ShapeDtypeStruct((tiles, size), f32),
    )
    results = pl.pallas_call(
        functools.partial(kernel, gx, gy, tiles, size, rows),
        out_shape=shapes,
        in_specs=[hbm] * 6 + [pl.BlockSpec(memory_space=pltpu.SMEM)],
        out_specs=(vmem,) * 3,
        scratch_shapes=[
            pltpu.VMEM((3, tiles, size), f32),
            pltpu.VMEM((tiles, size), f32),
            pltpu.VMEM((1, tiles), jnp.int32),
            pltpu.VMEM((2, rows), jnp.int32),
            pltpu.SemaphoreType.DMA((6,)),
            pltpu.VMEM((BOXES, 4, tiles, size), f32),
            pltpu.VMEM((BOXES, 4, tiles, size), f32),
            pltpu.VMEM((KDEPTH * (all_tiles + 1), size), f32),
            pltpu.VMEM((KDEPTH * (all_tiles + 1), size), f32),
            pltpu.VMEM((8 * (all_tiles + 1), size), f32),
            pltpu.VMEM((2 * FEATURES * (all_tiles + 1), size), f32),
            pltpu.VMEM((UNROLL, size, size), f32),
            pltpu.VMEM((UNROLL, 2 * size, size), bf16),
            pltpu.VMEM((rows, size, size), f32),
            pltpu.VMEM((rows, 2 * size, size), bf16),
            pltpu.VMEM((3 * rows + 16, size), f32),
            pltpu.VMEM((FEATURES * (2 * rows + 1), size), f32),
            pltpu.VMEM((all_tiles, 2 * rows), bf16),
            pltpu.VMEM((2, rows), jnp.int32),
            pltpu.SMEM((2, rows), jnp.int32),
            pltpu.SemaphoreType.DMA,
            pltpu.VMEM((BOXES, tiles, size), f32),
            pltpu.VMEM((BOXES, tiles, size), f32),
            pltpu.VMEM((BOXES, tiles, size), f32),
            pltpu.VMEM((BOXES, 3, tiles, size), f32),
            pltpu.VMEM((BOXES, 3, tiles, size), f32),
            pltpu.SemaphoreType.DMA((5, BOXES)),
            pltpu.SemaphoreType.DMA((5, BOXES)),
        ],
        compiler_params=pltpu.CompilerParams(collective_id=0, has_side_effects=True, vmem_limit_bytes=40 << 20),
        name="sph_step",
    )(
        *(
            pltpu.with_memory_space_constraint(value, pltpu.HBM)
            for value in (
                points,
                speeds,
                mass.reshape(tiles, size),
                stiffness.reshape(tiles, size),
                counts.reshape(1, tiles),
                turned,
            )
        ),
        pair_count,
    )
    new_points, new_speeds, density = pl.pallas_call(
        store_kernel,
        out_shape=shapes,
        in_specs=[vmem] * 3,
        out_specs=(hbm,) * 3,
        scratch_shapes=[pltpu.SemaphoreType.DMA((3,))],
        compiler_params=pltpu.CompilerParams(vmem_limit_bytes=1 << 20),
        name="sph_store",
    )(*results)
    return (
        new_points.reshape(positions.shape),
        new_speeds.reshape(velocities.shape),
        density.reshape(mass.shape),
    )


def solution(mesh):
    placed = (
        P(None, "gx", "gy", None),
        P(None, "gx", "gy", None),
        P("gx", "gy", None),
        P("gx", "gy", None),
        P("gx", "gy", None),
        P(("gx", "gy"), None),
        P(("gx", "gy")),
    )
    return jax.shard_map(
        functools.partial(body, mesh.shape["gx"], mesh.shape["gy"]),
        mesh=mesh,
        in_specs=placed,
        out_specs=(P(None, "gx", "gy", None), P(None, "gx", "gy", None), P("gx", "gy", None)),
        check_vma=False,
    )
```

```python
import functools
import math

import jax
import jax.numpy as jnp
from jax import lax
from jax.experimental import pallas as pl
from jax.experimental.pallas import tpu as pltpu
from jax.sharding import PartitionSpec as P

kernel_norm = 21.0 / (16.0 * math.pi)
viscosity = 0.1
time_step = 0.02
rest_density = 1.0

MESH = pl.DeviceIdType.MESH
OWN = 2
BOXES = 5
BESIDE = (1, 3, 0, 4)
INWARD = (0, 4, 1, 3)
KDEPTH = 24
FEATURES = 16
UNROLL = 16
FORCE_UNROLL = 32

f32, bf16 = jnp.float32, jnp.bfloat16


def split_in(value, parts):
    pieces = []
    for _ in range(parts):
        piece = value.astype(bf16)
        pieces.append(piece)
        value = value - piece.astype(f32)
    return pieces


def dot_nn(a, b):
    return lax.dot_general(a, b, (((1,), (0,)), ((), ())), preferred_element_type=f32)


def dot_nt(a, b):
    return lax.dot_general(a, b, (((1,), (1,)), ((), ())), preferred_element_type=f32)


def kernel(
    gx, gy, tiles, size, rows,
    pos_h, vel_h, mass_h, stiff_h, counts_h, pairs_h, live_s,
    points_out, speeds_out, density_out,
    pos, mass, counts, pairs_v, in_sem,
    pm, vs, side_a, side_b, mass_rows, feats, squares, weights, falls, slope,
    row_density, force_high, force_low, picks, table_v, table_s, table_sem,
    dens_part, dens_recv, dens_total, force_part, force_recv, send_sem, recv_sem,
):
    my_x, my_y = lax.axis_index("gx"), lax.axis_index("gy")
    where_to = {
        0: (my_x - 1, my_y),
        1: (my_x, my_y - 1),
        3: (my_x, my_y + 1),
        4: (my_x + 1, my_y),
    }
    there = {0: my_x > 0, 1: my_y > 0, 3: my_y < gy - 1, 4: my_x < gx - 1}
    all_tiles = BOXES * tiles
    plane_step, force_step = all_tiles + 1, 2 * rows + tiles + 1

    barrier = pltpu.get_barrier_semaphore()
    for b in BESIDE:

        @pl.when(there[b])
        def _(b=b):
            pl.semaphore_signal(barrier, inc=1, device_id=where_to[b], device_id_type=MESH)


    inputs = (
        (pos_h, pos),
        (mass_h, mass),
        (counts_h, counts),
        (pairs_h, pairs_v),
        (vel_h, vs.at[OWN, 0:3]),
        (stiff_h, vs.at[OWN, 3]),
    )
    loads = [pltpu.make_async_copy(a, b, in_sem.at[k]) for k, (a, b) in enumerate(inputs)]
    for load in loads:
        load.start()

    for load in loads[0:3]:
        load.wait()
    row_at = lax.broadcasted_iota(jnp.int32, (tiles, tiles), 0)
    column_at = lax.broadcasted_iota(jnp.int32, (tiles, tiles), 1)
    count = jnp.sum(
        jnp.where(row_at == column_at, counts[...].astype(f32), 0.0), axis=1, keepdims=True
    )
    lane = lax.broadcasted_iota(jnp.int32, (tiles, size), 1).astype(f32)
    for c in range(3):
        pm[OWN, c] = 0.5 * (pos[c] - 1.0)
    pm[OWN, 3] = jnp.where(lane < count, mass[...], 0.0)

    pl.semaphore_wait(barrier, sum(there[b].astype(jnp.int32) for b in BESIDE))

    def copy_to(stage, b, source, target):
        return pltpu.make_async_remote_copy(
            src_ref=source,
            dst_ref=target.at[4 - b],
            send_sem=send_sem.at[stage, b],
            recv_sem=recv_sem.at[stage, 4 - b],
            device_id=where_to[b],
            device_id_type=MESH,
        )

    def send_to(stage, b, source, target):
        @pl.when(there[b])
        def _():
            copy_to(stage, b, source, target).start()

    def exchange(stage, source_of, target):
        for b in BESIDE:
            send_to(stage, b, source_of(b), target)
        return stage, source_of, target

    def arrived(stage, b, target):
        @pl.when(there[b])
        def _():
            pltpu.make_async_remote_copy(
                src_ref=target.at[b],
                dst_ref=target.at[b],
                send_sem=send_sem.at[stage, b],
                recv_sem=recv_sem.at[stage, b],
                device_id=where_to[b],
                device_id_type=MESH,
            ).wait_recv()

    sent = []
    sent.append(exchange(0, lambda b: pm.at[OWN], pm))

    def at_plane(ref, plane, b):
        return ref.at[pl.ds(plane * plane_step + b * tiles, tiles)]

    def distance_planes(b):
        ones = jnp.ones((tiles, size), f32)
        norm = jnp.zeros((tiles, size), f32)
        planes_a, planes_b = [], []
        for c in range(3):
            h = pm[b, c]
            norm = norm + h * h
            h1, h2, h3 = (p.astype(f32) for p in split_in(h, 3))
            planes_a += [-2.0 * v for v in (h1, h1, h2, h2, h1, h3)]
            planes_b += [h1, h2, h1, h2, h3, h1]
        n_parts = [p.astype(f32) for p in split_in(norm, 3)]
        planes_a += n_parts + [ones] * 3
        planes_b += [ones] * 3 + n_parts
        if b in (0, OWN, 4):
            for k, value in enumerate(planes_a):
                at_plane(side_a, k, b)[...] = value
        if b in (1, OWN, 3):
            for k, value in enumerate(planes_b):
                at_plane(side_b, k, b)[...] = value
        for k, value in enumerate(split_in(pm[b, 3], 2)):
            at_plane(mass_rows, k, b)[...] = value.astype(f32)

    for start in (0, rows):
        row_density[pl.ds(start, tiles)] = jnp.zeros((tiles, size), f32)
    loads[3].wait()
    first = pairs_v[0:1, :]
    second = pairs_v[1:2, :]
    row_index = lax.broadcasted_iota(jnp.int32, (1, rows), 1)
    live = (row_index < live_s[0]) & (row_index >= tiles)

    first_tile = (OWN + 2 * (lax.div(first, gy * tiles) - my_x)) * tiles + lax.rem(first, tiles)
    second_tile = (OWN + lax.rem(lax.div(second, tiles), gy) - my_y) * tiles + lax.rem(second, tiles)
    to_first = jnp.where(live, first_tile, -1)
    to_second = jnp.where(live & (first != second), second_tile, -1)
    tile_at = lax.broadcasted_iota(jnp.int32, (all_tiles, rows), 0)
    picks[:, 0:rows] = jnp.where(tile_at == to_first, 1.0, 0.0).astype(bf16)
    picks[:, rows : 2 * rows] = jnp.where(tile_at == to_second, 1.0, 0.0).astype(bf16)
    table_v[0:1] = jnp.clip(first_tile, 0, all_tiles - 1)
    table_v[1:2] = jnp.clip(second_tile, 0, all_tiles - 1)
    table_copy = pltpu.make_async_copy(table_v, table_s, table_sem)
    table_copy.start()
    distance_planes(OWN)

    def own_tiles(r):
        return OWN * tiles + r, OWN * tiles + r

    def listed_tiles(r):
        return table_s[0, r], table_s[1, r]

    def tile_rows(ref, tile, count):
        return ref[pl.ds(tile, count, stride=plane_step), :].astype(bf16)

    def twice(value):
        return jnp.concatenate([value, value], axis=1)

    def side_by_side(value):
        return jnp.concatenate([value[0:size], value[size : 2 * size]], axis=1)

    def distances(u, one, two):
        def stacked(ref, tile):
            return ref[pl.ds(tile, KDEPTH, stride=plane_step), :]

        a = jnp.concatenate([stacked(side_a, one[0]), stacked(side_a, two[0])], axis=0)
        none = jnp.zeros((KDEPTH, size), f32)
        left = jnp.concatenate([stacked(side_b, one[1]), none], axis=0)
        right = jnp.concatenate([none, stacked(side_b, two[1])], axis=0)
        b = jnp.concatenate([left.astype(bf16), right.astype(bf16)], axis=1)
        both = lax.dot_general(
            a.astype(bf16), b, (((0,), (0,)), ((), ())), preferred_element_type=f32
        )
        squares[u] = both[:, 0:size]
        squares[u + 1] = both[:, size:]

    def weigh(r, u):
        square = lax.clamp(1e-13, squares[u], 1.0)
        fall = 1.0 - square * lax.rsqrt(square)
        fall2 = fall * fall
        falls[r] = fall
        weight_hi, weight_lo = split_in(fall2 * fall2 * (1.25 - fall), 2)
        weights[u, 0:size] = weight_hi
        weights[u, size : 2 * size] = weight_lo

    def add_up(r, u, t1, t2, cross):
        both = weights[u]
        got = dot_nt(twice(tile_rows(mass_rows, t2, 8)), side_by_side(both))
        row_density[pl.ds(r if cross else 2 * rows + r, 1)] = got[0:1] + got[1:2]
        if cross:
            got = dot_nn(twice(tile_rows(mass_rows, t1, 8)), both)
            row_density[pl.ds(rows + r, 1)] = got[0:1] + got[1:2]

    def density_rows(start, end, tiles_of, cross):
        for u in range(0, UNROLL, 2):
            distances(u, tiles_of(start + u), tiles_of(start + u + 1))

        def turn(step, carry):
            for u in range(UNROLL):
                r = start + step * UNROLL + u
                before = jnp.maximum(r - UNROLL, start)
                spare = jnp.where(step == 0, (2 * rows if cross else 0) + tiles + u, before)
                add_up(spare, u, *tiles_of(before), cross)
                weigh(r, u)
                if u % 2:
                    ahead = jnp.minimum(r + UNROLL, end - 1)
                    distances(u - 1, tiles_of(ahead - 1), tiles_of(ahead))
            return carry

        lax.fori_loop(0, (end - start) // UNROLL, turn, 0)
        for u in range(UNROLL):
            r = end - UNROLL + u
            add_up(r, u, *tiles_of(r), cross)

    def slopes(start, end):
        def turn(step, carry):
            for u in range(4):
                r = start + step * 4 + u
                fall = falls[r]
                slope_hi, slope_lo = split_in(fall * fall * fall, 2)
                slope[r, 0:size] = slope_hi
                slope[r, size : 2 * size] = slope_lo
            return carry

        lax.fori_loop(0, (end - start) // 4, turn, 0)

    def keep_sums(row, got):
        value = got[0:FEATURES] + got[FEATURES:]
        high, low = (piece.astype(f32) for piece in split_in(value, 2))
        force_high[pl.ds(row, FEATURES, stride=force_step), :] = high
        force_low[pl.ds(row, FEATURES, stride=force_step), :] = low

    def force_row(r, t1, t2, cross):
        both = slope[r]
        got = dot_nt(twice(tile_rows(feats, t2, 2 * FEATURES)), side_by_side(both))
        keep_sums(r if cross else 2 * rows + r, got)
        if cross:
            keep_sums(rows + r, dot_nn(twice(tile_rows(feats, t1, 2 * FEATURES)), both))

    def force_rows(start, end, tiles_of, cross, unroll=FORCE_UNROLL):
        def turn(step, carry):
            for u in range(unroll):
                r = start + step * unroll + u
                force_row(r, *tiles_of(r), cross)
            return carry

        lax.fori_loop(0, (end - start) // unroll, turn, 0)

    table_copy.wait()
    for b in INWARD:
        arrived(0, b, pm)
        distance_planes(b)
    for load in loads[4:6]:
        load.wait()
    sent.append(exchange(1, lambda b: vs.at[OWN], vs))
    density_rows(tiles, rows, listed_tiles, True)

    chosen = picks[...]
    total = jnp.zeros((all_tiles, size), f32)
    for part in split_in(row_density[0 : 2 * rows], 3):
        total = total + dot_nn(chosen, part)
    dens_part[...] = ((4.0 * kernel_norm) * total).reshape(BOXES, tiles, size)
    sent.append(exchange(2, lambda b: dens_part.at[b], dens_recv))
    density_rows(0, tiles, own_tiles, False)
    slopes(0, rows // 2)
    for ref in (force_high, force_low):
        for f in range(12):
            for start in (0, rows):
                ref[pl.ds(f * force_step + start, tiles)] = jnp.zeros((tiles, size), f32)
    density = dens_part[OWN] + (4.0 * kernel_norm) * row_density[2 * rows : 2 * rows + tiles]
    for b in INWARD:
        arrived(2, b, dens_recv)
        density = density + jnp.where(there[b], dens_recv[b], 0.0)
    dens_total[OWN] = density
    density_out[...] = density
    sent.append(exchange(3, lambda b: dens_total.at[OWN], dens_total))

    def pressures(b):
        density = dens_total[b]
        scale = density + 1.0 - jnp.where(pm[b, 3] > 0.0, 1.0, 0.0)
        inverse = 1.0 / scale
        press = vs[b, 3] * (density - rest_density) * inverse * inverse
        return press, inverse

    def force_planes(b):
        press, inverse = pressures(b)
        m = pm[b, 3]
        mp, mq = m * press, m * inverse
        values = [m] + [m * pm[b, c] for c in range(3)]
        values += [mp] + [mp * pm[b, c] for c in range(3)]
        values += [mq] + [mq * vs[b, c] for c in range(3)]
        for k, value in enumerate(values):
            for part, piece in enumerate(split_in(value, 2)):
                at_plane(feats, part * FEATURES + k, b)[...] = piece.astype(f32)

    slopes(rows // 2, rows)
    force_planes(OWN)
    force_rows(0, tiles, own_tiles, False)
    for b in INWARD:
        arrived(1, b, vs)
        arrived(3, b, dens_total)
        force_planes(b)
    force_rows(tiles, rows, listed_tiles, True, 48)

    sums = []
    for f in range(0, 12, 2):
        total = jnp.zeros((all_tiles, 2 * size), f32)
        for ref in (force_high, force_low):
            pair = [ref[pl.ds((f + k) * force_step, 2 * rows)].astype(bf16) for k in range(2)]
            total = total + dot_nn(chosen, jnp.concatenate(pair, axis=1))
        sums += [total[:, 0:size], total[:, size:]]
    sent.append((4, lambda b: force_part.at[b], force_recv))
    for b in BESIDE + (OWN,):
        press, inverse = pressures(b)
        s = [v[b * tiles : (b + 1) * tiles] for v in sums]
        if b == OWN:
            for f in range(12):
                own = pl.ds(f * force_step + 2 * rows, tiles)
                s[f] = s[f] + force_high[own] + force_low[own]
        for c in range(3):
            h, v = pm[b, c], vs[b, c]
            push = press * (h * s[0] - s[1 + c]) + h * s[4] - s[5 + c]
            drag = inverse * (v * s[8] - s[9 + c])
            force_part[b, c] = (5.0 * kernel_norm) * (2.0 * push - (2.0 * viscosity) * drag)
        if b != OWN:
            send_to(4, b, force_part.at[b], force_recv)
    accel = force_part[OWN]
    for b in INWARD:
        arrived(4, b, force_recv)
        accel = accel + jnp.where(there[b], force_recv[b], 0.0)
    accel = accel * jnp.where(pm[OWN, 3] > 0.0, 1.0, 0.0)[None]
    new_speeds = vs[OWN, 0:3] + time_step * accel
    speeds_out[...] = new_speeds
    points_out[...] = pos[...] + time_step * new_speeds

    for stage, source_of, target in sent:
        for b in BESIDE:

            @pl.when(there[b])
            def _(b=b):
                copy_to(stage, b, source_of(b), target).wait_send()


def store_kernel(points, speeds, density, points_out, speeds_out, density_out, sem):
    pairs = ((points, points_out), (speeds, speeds_out), (density, density_out))
    stores = [pltpu.make_async_copy(a, b, sem.at[k]) for k, (a, b) in enumerate(pairs)]
    for store in stores:
        store.start()
    for store in stores:
        store.wait()


def body(gx, gy, positions, velocities, mass, stiffness, counts, pairs, pair_count):
    tiles = counts.shape[2]
    size = positions.shape[3] // tiles
    rows = pairs.shape[0]
    all_tiles = BOXES * tiles
    points = positions.reshape(3, tiles, size)
    speeds = velocities.reshape(3, tiles, size)
    turned = pairs.T
    vmem = pl.BlockSpec(memory_space=pltpu.VMEM)
    hbm = pl.BlockSpec(memory_space=pltpu.HBM)
    shapes = (
        jax.ShapeDtypeStruct((3, tiles, size), f32),
        jax.ShapeDtypeStruct((3, tiles, size), f32),
        jax.ShapeDtypeStruct((tiles, size), f32),
    )
    results = pl.pallas_call(
        functools.partial(kernel, gx, gy, tiles, size, rows),
        out_shape=shapes,
        in_specs=[hbm] * 6 + [pl.BlockSpec(memory_space=pltpu.SMEM)],
        out_specs=(vmem,) * 3,
        scratch_shapes=[
            pltpu.VMEM((3, tiles, size), f32),
            pltpu.VMEM((tiles, size), f32),
            pltpu.VMEM((1, tiles), jnp.int32),
            pltpu.VMEM((2, rows), jnp.int32),
            pltpu.SemaphoreType.DMA((6,)),
            pltpu.VMEM((BOXES, 4, tiles, size), f32),
            pltpu.VMEM((BOXES, 4, tiles, size), f32),
            pltpu.VMEM((KDEPTH * (all_tiles + 1), size), f32),
            pltpu.VMEM((KDEPTH * (all_tiles + 1), size), f32),
            pltpu.VMEM((8 * (all_tiles + 1), size), f32),
            pltpu.VMEM((2 * FEATURES * (all_tiles + 1), size), f32),
            pltpu.VMEM((UNROLL, size, size), f32),
            pltpu.VMEM((UNROLL, 2 * size, size), bf16),
            pltpu.VMEM((rows, size, size), f32),
            pltpu.VMEM((rows, 2 * size, size), bf16),
            pltpu.VMEM((3 * rows + 2 * tiles + 16, size), f32),
            pltpu.VMEM((FEATURES * (2 * rows + tiles + 1), size), f32),
            pltpu.VMEM((FEATURES * (2 * rows + tiles + 1), size), f32),
            pltpu.VMEM((all_tiles, 2 * rows), bf16),
            pltpu.VMEM((2, rows), jnp.int32),
            pltpu.SMEM((2, rows), jnp.int32),
            pltpu.SemaphoreType.DMA,
            pltpu.VMEM((BOXES, tiles, size), f32),
            pltpu.VMEM((BOXES, tiles, size), f32),
            pltpu.VMEM((BOXES, tiles, size), f32),
            pltpu.VMEM((BOXES, 3, tiles, size), f32),
            pltpu.VMEM((BOXES, 3, tiles, size), f32),
            pltpu.SemaphoreType.DMA((5, BOXES)),
            pltpu.SemaphoreType.DMA((5, BOXES)),
        ],
        compiler_params=pltpu.CompilerParams(collective_id=0, has_side_effects=True, vmem_limit_bytes=40 << 20),
        name="sph_step",
    )(
        *(
            pltpu.with_memory_space_constraint(value, pltpu.HBM)
            for value in (
                points,
                speeds,
                mass.reshape(tiles, size),
                stiffness.reshape(tiles, size),
                counts.reshape(1, tiles),
                turned,
            )
        ),
        pair_count,
    )
    new_points, new_speeds, density = pl.pallas_call(
        store_kernel,
        out_shape=shapes,
        in_specs=[vmem] * 3,
        out_specs=(hbm,) * 3,
        scratch_shapes=[pltpu.SemaphoreType.DMA((3,))],
        compiler_params=pltpu.CompilerParams(vmem_limit_bytes=1 << 20),
        name="sph_store",
    )(*results)
    return (
        new_points.reshape(positions.shape),
        new_speeds.reshape(velocities.shape),
        density.reshape(mass.shape),
    )


def solution(mesh):
    placed = (
        P(None, "gx", "gy", None),
        P(None, "gx", "gy", None),
        P("gx", "gy", None),
        P("gx", "gy", None),
        P("gx", "gy", None),
        P(("gx", "gy"), None),
        P(("gx", "gy")),
    )
    return jax.shard_map(
        functools.partial(body, mesh.shape["gx"], mesh.shape["gy"]),
        mesh=mesh,
        in_specs=placed,
        out_specs=(P(None, "gx", "gy", None), P(None, "gx", "gy", None), P("gx", "gy", None)),
        check_vma=False,
    )
```

```python
import functools
import math

import jax
import jax.numpy as jnp
from jax import lax
from jax.experimental import pallas as pl
from jax.experimental.pallas import tpu as pltpu
from jax.sharding import PartitionSpec as P

kernel_norm = 21.0 / (16.0 * math.pi)
viscosity = 0.1
time_step = 0.02
rest_density = 1.0

MESH = pl.DeviceIdType.MESH
OWN = 2
BOXES = 5
BESIDE = (1, 3, 0, 4)
INWARD = (0, 4, 1, 3)
KDEPTH = 24
FEATURES = 16
UNROLL = 16
FORCE_UNROLL = 32

f32, bf16 = jnp.float32, jnp.bfloat16


def split_in(value, parts):
    pieces = []
    for _ in range(parts):
        piece = value.astype(bf16)
        pieces.append(piece)
        value = value - piece.astype(f32)
    return pieces


def dot_nn(a, b):
    return lax.dot_general(a, b, (((1,), (0,)), ((), ())), preferred_element_type=f32)


def dot_nt(a, b):
    return lax.dot_general(a, b, (((1,), (1,)), ((), ())), preferred_element_type=f32)


def kernel(
    gx, gy, tiles, size, rows,
    pos_h, vel_h, mass_h, stiff_h, counts_h, pairs_h, live_s,
    points_out, speeds_out, density_out,
    pos, mass, counts, pairs_v, in_sem,
    pm, vs, side_a, side_b, mass_rows, feats, squares, weights, falls, slope,
    row_density, force_high, force_low, picks, table_v, table_s, table_sem,
    dens_part, dens_recv, dens_total, force_part, force_recv, send_sem, recv_sem,
):
    my_x, my_y = lax.axis_index("gx"), lax.axis_index("gy")
    where_to = {
        0: (my_x - 1, my_y),
        1: (my_x, my_y - 1),
        3: (my_x, my_y + 1),
        4: (my_x + 1, my_y),
    }
    there = {0: my_x > 0, 1: my_y > 0, 3: my_y < gy - 1, 4: my_x < gx - 1}
    all_tiles = BOXES * tiles
    plane_step, force_step = all_tiles + 1, 2 * rows + tiles + 1

    barrier = pltpu.get_barrier_semaphore()
    for b in BESIDE:

        @pl.when(there[b])
        def _(b=b):
            pl.semaphore_signal(barrier, inc=1, device_id=where_to[b], device_id_type=MESH)


    inputs = (
        (pos_h, pos),
        (mass_h, mass),
        (counts_h, counts),
        (pairs_h, pairs_v),
        (vel_h, vs.at[OWN, 0:3]),
        (stiff_h, vs.at[OWN, 3]),
    )
    loads = [pltpu.make_async_copy(a, b, in_sem.at[k]) for k, (a, b) in enumerate(inputs)]
    for load in loads:
        load.start()

    for load in loads[0:3]:
        load.wait()
    row_at = lax.broadcasted_iota(jnp.int32, (tiles, tiles), 0)
    column_at = lax.broadcasted_iota(jnp.int32, (tiles, tiles), 1)
    count = jnp.sum(
        jnp.where(row_at == column_at, counts[...].astype(f32), 0.0), axis=1, keepdims=True
    )
    lane = lax.broadcasted_iota(jnp.int32, (tiles, size), 1).astype(f32)
    for c in range(3):
        pm[OWN, c] = 0.5 * (pos[c] - 1.0)
    pm[OWN, 3] = jnp.where(lane < count, mass[...], 0.0)

    pl.semaphore_wait(barrier, sum(there[b].astype(jnp.int32) for b in BESIDE))

    def copy_to(stage, b, source, target):
        return pltpu.make_async_remote_copy(
            src_ref=source,
            dst_ref=target.at[4 - b],
            send_sem=send_sem.at[stage, b],
            recv_sem=recv_sem.at[stage, 4 - b],
            device_id=where_to[b],
            device_id_type=MESH,
        )

    def send_to(stage, b, source, target):
        @pl.when(there[b])
        def _():
            copy_to(stage, b, source, target).start()

    def exchange(stage, source_of, target):
        for b in BESIDE:
            send_to(stage, b, source_of(b), target)
        return stage, source_of, target

    def arrived(stage, b, target):
        @pl.when(there[b])
        def _():
            pltpu.make_async_remote_copy(
                src_ref=target.at[b],
                dst_ref=target.at[b],
                send_sem=send_sem.at[stage, b],
                recv_sem=recv_sem.at[stage, b],
                device_id=where_to[b],
                device_id_type=MESH,
            ).wait_recv()

    sent = []
    sent.append(exchange(0, lambda b: pm.at[OWN], pm))

    def at_plane(ref, plane, b):
        return ref.at[pl.ds(plane * plane_step + b * tiles, tiles)]

    def distance_planes(b):
        ones = jnp.ones((tiles, size), f32)
        norm = jnp.zeros((tiles, size), f32)
        planes_a, planes_b = [], []
        for c in range(3):
            h = pm[b, c]
            norm = norm + h * h
            h1, h2, h3 = (p.astype(f32) for p in split_in(h, 3))
            planes_a += [-2.0 * v for v in (h1, h1, h2, h2, h1, h3)]
            planes_b += [h1, h2, h1, h2, h3, h1]
        n_parts = [p.astype(f32) for p in split_in(norm, 3)]
        planes_a += n_parts + [ones] * 3
        planes_b += [ones] * 3 + n_parts
        if b in (0, OWN, 4):
            for k, value in enumerate(planes_a):
                at_plane(side_a, k, b)[...] = value
        if b in (1, OWN, 3):
            for k, value in enumerate(planes_b):
                at_plane(side_b, k, b)[...] = value
        for k, value in enumerate(split_in(pm[b, 3], 2)):
            at_plane(mass_rows, k, b)[...] = value.astype(f32)

    for start in (0, rows):
        row_density[pl.ds(start, tiles)] = jnp.zeros((tiles, size), f32)
    loads[3].wait()
    first = pairs_v[0:1, :]
    second = pairs_v[1:2, :]
    row_index = lax.broadcasted_iota(jnp.int32, (1, rows), 1)
    live = (row_index < live_s[0]) & (row_index >= tiles)

    first_tile = (OWN + 2 * (lax.div(first, gy * tiles) - my_x)) * tiles + lax.rem(first, tiles)
    second_tile = (OWN + lax.rem(lax.div(second, tiles), gy) - my_y) * tiles + lax.rem(second, tiles)
    to_first = jnp.where(live, first_tile, -1)
    to_second = jnp.where(live & (first != second), second_tile, -1)
    tile_at = lax.broadcasted_iota(jnp.int32, (all_tiles, rows), 0)
    picks[:, 0:rows] = jnp.where(tile_at == to_first, 1.0, 0.0).astype(bf16)
    picks[:, rows : 2 * rows] = jnp.where(tile_at == to_second, 1.0, 0.0).astype(bf16)
    table_v[0:1] = jnp.clip(first_tile, 0, all_tiles - 1)
    table_v[1:2] = jnp.clip(second_tile, 0, all_tiles - 1)
    table_copy = pltpu.make_async_copy(table_v, table_s, table_sem)
    table_copy.start()
    distance_planes(OWN)

    def own_tiles(r):
        return OWN * tiles + r, OWN * tiles + r

    def listed_tiles(r):
        return table_s[0, r], table_s[1, r]

    def tile_rows(ref, tile, count):
        return ref[pl.ds(tile, count, stride=plane_step), :].astype(bf16)

    def twice(value):
        return jnp.concatenate([value, value], axis=1)

    def side_by_side(value):
        return jnp.concatenate([value[0:size], value[size : 2 * size]], axis=1)

    def distances(u, one, two):
        def stacked(ref, tile):
            return ref[pl.ds(tile, KDEPTH, stride=plane_step), :]

        a = jnp.concatenate([stacked(side_a, one[0]), stacked(side_a, two[0])], axis=0)
        none = jnp.zeros((KDEPTH, size), f32)
        left = jnp.concatenate([stacked(side_b, one[1]), none], axis=0)
        right = jnp.concatenate([none, stacked(side_b, two[1])], axis=0)
        b = jnp.concatenate([left.astype(bf16), right.astype(bf16)], axis=1)
        both = lax.dot_general(
            a.astype(bf16), b, (((0,), (0,)), ((), ())), preferred_element_type=f32
        )
        squares[u] = both[:, 0:size]
        squares[u + 1] = both[:, size:]

    def weigh(r, u):
        square = lax.clamp(1e-13, squares[u], 1.0)
        fall = 1.0 - square * lax.rsqrt(square)
        fall2 = fall * fall
        falls[r] = fall
        weight_hi, weight_lo = split_in(fall2 * fall2 * (1.25 - fall), 2)
        weights[u, 0:size] = weight_hi
        weights[u, size : 2 * size] = weight_lo

    def add_up(r, u, t1, t2, cross):
        both = weights[u]
        got = dot_nt(twice(tile_rows(mass_rows, t2, 8)), side_by_side(both))
        row_density[pl.ds(r if cross else 2 * rows + r, 1)] = got[0:1] + got[1:2]
        if cross:
            got = dot_nn(twice(tile_rows(mass_rows, t1, 8)), both)
            row_density[pl.ds(rows + r, 1)] = got[0:1] + got[1:2]

    def density_rows(start, end, tiles_of, cross):
        for u in range(0, UNROLL, 2):
            distances(u, tiles_of(start + u), tiles_of(start + u + 1))

        def turn(step, carry):
            for u in range(UNROLL):
                r = start + step * UNROLL + u
                before = jnp.maximum(r - UNROLL, start)
                spare = jnp.where(step == 0, (2 * rows if cross else 0) + tiles + u, before)
                add_up(spare, u, *tiles_of(before), cross)
                weigh(r, u)
                if u % 2:
                    ahead = jnp.minimum(r + UNROLL, end - 1)
                    distances(u - 1, tiles_of(ahead - 1), tiles_of(ahead))
            return carry

        lax.fori_loop(0, (end - start) // UNROLL, turn, 0)
        for u in range(UNROLL):
            r = end - UNROLL + u
            add_up(r, u, *tiles_of(r), cross)

    def slopes(start, end):
        def turn(step, carry):
            for u in range(4):
                r = start + step * 4 + u
                fall = falls[r]
                slope_hi, slope_lo = split_in(fall * fall * fall, 2)
                slope[r, 0:size] = slope_hi
                slope[r, size : 2 * size] = slope_lo
            return carry

        lax.fori_loop(0, (end - start) // 4, turn, 0)

    def keep_sums(row, got):
        value = got[0:FEATURES] + got[FEATURES:]
        high, low = (piece.astype(f32) for piece in split_in(value, 2))
        force_high[pl.ds(row, FEATURES, stride=force_step), :] = high
        force_low[pl.ds(row, FEATURES, stride=force_step), :] = low

    def force_row(r, t1, t2, cross):
        both = slope[r]
        got = dot_nt(twice(tile_rows(feats, t2, 2 * FEATURES)), side_by_side(both))
        keep_sums(r if cross else 2 * rows + r, got)
        if cross:
            keep_sums(rows + r, dot_nn(twice(tile_rows(feats, t1, 2 * FEATURES)), both))

    def force_rows(start, end, tiles_of, cross, unroll=FORCE_UNROLL):
        def turn(step, carry):
            for u in range(unroll):
                r = start + step * unroll + u
                force_row(r, *tiles_of(r), cross)
            return carry

        lax.fori_loop(0, (end - start) // unroll, turn, 0)

    density_rows(0, tiles, own_tiles, False)
    slopes(0, tiles)
    table_copy.wait()
    for b in INWARD:
        arrived(0, b, pm)
        distance_planes(b)
    for load in loads[4:6]:
        load.wait()
    sent.append(exchange(1, lambda b: vs.at[OWN], vs))
    density_rows(tiles, rows, listed_tiles, True)

    chosen = picks[...]
    total = jnp.zeros((all_tiles, size), f32)
    for part in split_in(row_density[0 : 2 * rows], 3):
        total = total + dot_nn(chosen, part)
    dens_part[...] = ((4.0 * kernel_norm) * total).reshape(BOXES, tiles, size)
    sent.append(exchange(2, lambda b: dens_part.at[b], dens_recv))
    slopes(tiles, 3 * rows // 4)
    for ref in (force_high, force_low):
        for f in range(12):
            for start in (0, rows):
                ref[pl.ds(f * force_step + start, tiles)] = jnp.zeros((tiles, size), f32)
    density = dens_part[OWN] + (4.0 * kernel_norm) * row_density[2 * rows : 2 * rows + tiles]
    for b in INWARD:
        arrived(2, b, dens_recv)
        density = density + jnp.where(there[b], dens_recv[b], 0.0)
    dens_total[OWN] = density
    density_out[...] = density
    sent.append(exchange(3, lambda b: dens_total.at[OWN], dens_total))

    def pressures(b):
        density = dens_total[b]
        scale = density + 1.0 - jnp.where(pm[b, 3] > 0.0, 1.0, 0.0)
        inverse = 1.0 / scale
        press = vs[b, 3] * (density - rest_density) * inverse * inverse
        return press, inverse

    def force_planes(b):
        press, inverse = pressures(b)
        m = pm[b, 3]
        mp, mq = m * press, m * inverse
        values = [m] + [m * pm[b, c] for c in range(3)]
        values += [mp] + [mp * pm[b, c] for c in range(3)]
        values += [mq] + [mq * vs[b, c] for c in range(3)]
        for k, value in enumerate(values):
            for part, piece in enumerate(split_in(value, 2)):
                at_plane(feats, part * FEATURES + k, b)[...] = piece.astype(f32)

    slopes(3 * rows // 4, rows)
    force_planes(OWN)
    force_rows(0, tiles, own_tiles, False)
    for b in INWARD:
        arrived(1, b, vs)
        arrived(3, b, dens_total)
        force_planes(b)
    force_rows(tiles, rows, listed_tiles, True, 48)

    sums = []
    for f in range(0, 12, 2):
        total = jnp.zeros((all_tiles, 2 * size), f32)
        for ref in (force_high, force_low):
            pair = [ref[pl.ds((f + k) * force_step, 2 * rows)].astype(bf16) for k in range(2)]
            total = total + dot_nn(chosen, jnp.concatenate(pair, axis=1))
        sums += [total[:, 0:size], total[:, size:]]
    sent.append((4, lambda b: force_part.at[b], force_recv))
    for b in BESIDE + (OWN,):
        press, inverse = pressures(b)
        s = [v[b * tiles : (b + 1) * tiles] for v in sums]
        if b == OWN:
            for f in range(12):
                own = pl.ds(f * force_step + 2 * rows, tiles)
                s[f] = s[f] + force_high[own] + force_low[own]
        for c in range(3):
            h, v = pm[b, c], vs[b, c]
            push = press * (h * s[0] - s[1 + c]) + h * s[4] - s[5 + c]
            drag = inverse * (v * s[8] - s[9 + c])
            force_part[b, c] = (5.0 * kernel_norm) * (2.0 * push - (2.0 * viscosity) * drag)
        if b != OWN:
            send_to(4, b, force_part.at[b], force_recv)
    accel = force_part[OWN]
    for b in INWARD:
        arrived(4, b, force_recv)
        accel = accel + jnp.where(there[b], force_recv[b], 0.0)
    accel = accel * jnp.where(pm[OWN, 3] > 0.0, 1.0, 0.0)[None]
    new_speeds = vs[OWN, 0:3] + time_step * accel
    speeds_out[...] = new_speeds
    points_out[...] = pos[...] + time_step * new_speeds

    for stage, source_of, target in sent:
        for b in BESIDE:

            @pl.when(there[b])
            def _(b=b):
                copy_to(stage, b, source_of(b), target).wait_send()


def store_kernel(points, speeds, density, points_out, speeds_out, density_out, sem):
    pairs = ((points, points_out), (speeds, speeds_out), (density, density_out))
    stores = [pltpu.make_async_copy(a, b, sem.at[k]) for k, (a, b) in enumerate(pairs)]
    for store in stores:
        store.start()
    for store in stores:
        store.wait()


def body(gx, gy, positions, velocities, mass, stiffness, counts, pairs, pair_count):
    tiles = counts.shape[2]
    size = positions.shape[3] // tiles
    rows = pairs.shape[0]
    all_tiles = BOXES * tiles
    points = positions.reshape(3, tiles, size)
    speeds = velocities.reshape(3, tiles, size)
    turned = pairs.T
    vmem = pl.BlockSpec(memory_space=pltpu.VMEM)
    hbm = pl.BlockSpec(memory_space=pltpu.HBM)
    shapes = (
        jax.ShapeDtypeStruct((3, tiles, size), f32),
        jax.ShapeDtypeStruct((3, tiles, size), f32),
        jax.ShapeDtypeStruct((tiles, size), f32),
    )
    results = pl.pallas_call(
        functools.partial(kernel, gx, gy, tiles, size, rows),
        out_shape=shapes,
        in_specs=[hbm] * 6 + [pl.BlockSpec(memory_space=pltpu.SMEM)],
        out_specs=(vmem,) * 3,
        scratch_shapes=[
            pltpu.VMEM((3, tiles, size), f32),
            pltpu.VMEM((tiles, size), f32),
            pltpu.VMEM((1, tiles), jnp.int32),
            pltpu.VMEM((2, rows), jnp.int32),
            pltpu.SemaphoreType.DMA((6,)),
            pltpu.VMEM((BOXES, 4, tiles, size), f32),
            pltpu.VMEM((BOXES, 4, tiles, size), f32),
            pltpu.VMEM((KDEPTH * (all_tiles + 1), size), f32),
            pltpu.VMEM((KDEPTH * (all_tiles + 1), size), f32),
            pltpu.VMEM((8 * (all_tiles + 1), size), f32),
            pltpu.VMEM((2 * FEATURES * (all_tiles + 1), size), f32),
            pltpu.VMEM((UNROLL, size, size), f32),
            pltpu.VMEM((UNROLL, 2 * size, size), bf16),
            pltpu.VMEM((rows, size, size), f32),
            pltpu.VMEM((rows, 2 * size, size), bf16),
            pltpu.VMEM((3 * rows + 2 * tiles + 16, size), f32),
            pltpu.VMEM((FEATURES * (2 * rows + tiles + 1), size), f32),
            pltpu.VMEM((FEATURES * (2 * rows + tiles + 1), size), f32),
            pltpu.VMEM((all_tiles, 2 * rows), bf16),
            pltpu.VMEM((2, rows), jnp.int32),
            pltpu.SMEM((2, rows), jnp.int32),
            pltpu.SemaphoreType.DMA,
            pltpu.VMEM((BOXES, tiles, size), f32),
            pltpu.VMEM((BOXES, tiles, size), f32),
            pltpu.VMEM((BOXES, tiles, size), f32),
            pltpu.VMEM((BOXES, 3, tiles, size), f32),
            pltpu.VMEM((BOXES, 3, tiles, size), f32),
            pltpu.SemaphoreType.DMA((5, BOXES)),
            pltpu.SemaphoreType.DMA((5, BOXES)),
        ],
        compiler_params=pltpu.CompilerParams(collective_id=0, has_side_effects=True, vmem_limit_bytes=40 << 20),
        name="sph_step",
    )(
        *(
            pltpu.with_memory_space_constraint(value, pltpu.HBM)
            for value in (
                points,
                speeds,
                mass.reshape(tiles, size),
                stiffness.reshape(tiles, size),
                counts.reshape(1, tiles),
                turned,
            )
        ),
        pair_count,
    )
    new_points, new_speeds, density = pl.pallas_call(
        store_kernel,
        out_shape=shapes,
        in_specs=[vmem] * 3,
        out_specs=(hbm,) * 3,
        scratch_shapes=[pltpu.SemaphoreType.DMA((3,))],
        compiler_params=pltpu.CompilerParams(vmem_limit_bytes=1 << 20),
        name="sph_store",
    )(*results)
    return (
        new_points.reshape(positions.shape),
        new_speeds.reshape(velocities.shape),
        density.reshape(mass.shape),
    )


def solution(mesh):
    placed = (
        P(None, "gx", "gy", None),
        P(None, "gx", "gy", None),
        P("gx", "gy", None),
        P("gx", "gy", None),
        P("gx", "gy", None),
        P(("gx", "gy"), None),
        P(("gx", "gy")),
    )
    return jax.shard_map(
        functools.partial(body, mesh.shape["gx"], mesh.shape["gy"]),
        mesh=mesh,
        in_specs=placed,
        out_specs=(P(None, "gx", "gy", None), P(None, "gx", "gy", None), P("gx", "gy", None)),
        check_vma=False,
    )
```

```python
import functools
import math

import jax
import jax.numpy as jnp
from jax import lax
from jax.experimental import pallas as pl
from jax.experimental.pallas import tpu as pltpu
from jax.sharding import PartitionSpec as P

kernel_norm = 21.0 / (16.0 * math.pi)
viscosity = 0.1
time_step = 0.02
rest_density = 1.0

MESH = pl.DeviceIdType.MESH
OWN = 2
BOXES = 5
BESIDE = (1, 3, 0, 4)
INWARD = (0, 4, 1, 3)
KDEPTH = 24
FEATURES = 16
UNROLL = 16
FORCE_UNROLL = 32

f32, bf16 = jnp.float32, jnp.bfloat16


def split_in(value, parts):
    pieces = []
    for _ in range(parts):
        piece = value.astype(bf16)
        pieces.append(piece)
        value = value - piece.astype(f32)
    return pieces


def dot_nn(a, b):
    return lax.dot_general(a, b, (((1,), (0,)), ((), ())), preferred_element_type=f32)


def dot_nt(a, b):
    return lax.dot_general(a, b, (((1,), (1,)), ((), ())), preferred_element_type=f32)


def kernel(
    gx, gy, tiles, size, rows,
    pos_h, vel_h, mass_h, stiff_h, counts_h, pairs_h, live_s,
    points_out, speeds_out, density_out,
    pos, mass, counts, pairs_v, in_sem,
    pm, vs, side_a, side_b, mass_rows, feats, squares, weights, falls, slope,
    row_density, force_high, force_low, picks, table_v, table_s, table_sem,
    dens_part, dens_recv, dens_total, force_part, force_recv, send_sem, recv_sem,
):
    my_x, my_y = lax.axis_index("gx"), lax.axis_index("gy")
    where_to = {
        0: (my_x - 1, my_y),
        1: (my_x, my_y - 1),
        3: (my_x, my_y + 1),
        4: (my_x + 1, my_y),
    }
    there = {0: my_x > 0, 1: my_y > 0, 3: my_y < gy - 1, 4: my_x < gx - 1}
    all_tiles = BOXES * tiles
    plane_step, force_step = all_tiles + 1, 2 * rows + tiles + 1

    barrier = pltpu.get_barrier_semaphore()
    for b in BESIDE:

        @pl.when(there[b])
        def _(b=b):
            pl.semaphore_signal(barrier, inc=1, device_id=where_to[b], device_id_type=MESH)


    inputs = (
        (pos_h, pos),
        (mass_h, mass),
        (counts_h, counts),
        (pairs_h, pairs_v),
        (vel_h, vs.at[OWN, 0:3]),
        (stiff_h, vs.at[OWN, 3]),
    )
    loads = [pltpu.make_async_copy(a, b, in_sem.at[k]) for k, (a, b) in enumerate(inputs)]
    for load in loads:
        load.start()

    for load in loads[0:3]:
        load.wait()
    row_at = lax.broadcasted_iota(jnp.int32, (tiles, tiles), 0)
    column_at = lax.broadcasted_iota(jnp.int32, (tiles, tiles), 1)
    count = jnp.sum(
        jnp.where(row_at == column_at, counts[...].astype(f32), 0.0), axis=1, keepdims=True
    )
    lane = lax.broadcasted_iota(jnp.int32, (tiles, size), 1).astype(f32)
    for c in range(3):
        pm[OWN, c] = 0.5 * (pos[c] - 1.0)
    pm[OWN, 3] = jnp.where(lane < count, mass[...], 0.0)

    pl.semaphore_wait(barrier, sum(there[b].astype(jnp.int32) for b in BESIDE))

    def copy_to(stage, b, source, target):
        return pltpu.make_async_remote_copy(
            src_ref=source,
            dst_ref=target(4 - b),
            send_sem=send_sem.at[stage, b],
            recv_sem=recv_sem.at[stage, 4 - b],
            device_id=where_to[b],
            device_id_type=MESH,
        )

    def send_to(stage, b, source, target):
        @pl.when(there[b])
        def _():
            copy_to(stage, b, source, target).start()

    def exchange(stage, source_of, target):
        for b in BESIDE:
            send_to(stage, b, source_of(b), target)
        return stage, source_of, target

    def arrived(stage, b, target):
        @pl.when(there[b])
        def _():
            pltpu.make_async_remote_copy(
                src_ref=target(b),
                dst_ref=target(b),
                send_sem=send_sem.at[stage, b],
                recv_sem=recv_sem.at[stage, b],
                device_id=where_to[b],
                device_id_type=MESH,
            ).wait_recv()

    def slot(ref):
        return lambda b: ref.at[b]

    def pos_of(b):
        return pm.at[b, 0:3]

    def mass_of(b):
        return pm.at[b, 3]

    sent = []
    sent.append(exchange(0, lambda b: pos_of(OWN), pos_of))
    sent.append(exchange(5, lambda b: mass_of(OWN), mass_of))

    def at_plane(ref, plane, b):
        return ref.at[pl.ds(plane * plane_step + b * tiles, tiles)]

    def distance_planes(b):
        ones = jnp.ones((tiles, size), f32)
        norm = jnp.zeros((tiles, size), f32)
        planes_a, planes_b = [], []
        for c in range(3):
            h = pm[b, c]
            norm = norm + h * h
            h1, h2, h3 = (p.astype(f32) for p in split_in(h, 3))
            planes_a += [-2.0 * v for v in (h1, h1, h2, h2, h1, h3)]
            planes_b += [h1, h2, h1, h2, h3, h1]
        n_parts = [p.astype(f32) for p in split_in(norm, 3)]
        planes_a += n_parts + [ones] * 3
        planes_b += [ones] * 3 + n_parts
        if b in (0, OWN, 4):
            for k, value in enumerate(planes_a):
                at_plane(side_a, k, b)[...] = value
        if b in (1, OWN, 3):
            for k, value in enumerate(planes_b):
                at_plane(side_b, k, b)[...] = value

    def mass_planes(b):
        for k, value in enumerate(split_in(pm[b, 3], 2)):
            at_plane(mass_rows, k, b)[...] = value.astype(f32)

    for start in (0, rows):
        row_density[pl.ds(start, tiles)] = jnp.zeros((tiles, size), f32)
    loads[3].wait()
    first = pairs_v[0:1, :]
    second = pairs_v[1:2, :]
    row_index = lax.broadcasted_iota(jnp.int32, (1, rows), 1)
    live = (row_index < live_s[0]) & (row_index >= tiles)

    first_tile = (OWN + 2 * (lax.div(first, gy * tiles) - my_x)) * tiles + lax.rem(first, tiles)
    second_tile = (OWN + lax.rem(lax.div(second, tiles), gy) - my_y) * tiles + lax.rem(second, tiles)
    to_first = jnp.where(live, first_tile, -1)
    to_second = jnp.where(live & (first != second), second_tile, -1)
    tile_at = lax.broadcasted_iota(jnp.int32, (all_tiles, rows), 0)
    picks[:, 0:rows] = jnp.where(tile_at == to_first, 1.0, 0.0).astype(bf16)
    picks[:, rows : 2 * rows] = jnp.where(tile_at == to_second, 1.0, 0.0).astype(bf16)
    table_v[0:1] = jnp.clip(first_tile, 0, all_tiles - 1)
    table_v[1:2] = jnp.clip(second_tile, 0, all_tiles - 1)
    table_copy = pltpu.make_async_copy(table_v, table_s, table_sem)
    table_copy.start()
    distance_planes(OWN)
    mass_planes(OWN)

    def own_tiles(r):
        return OWN * tiles + r, OWN * tiles + r

    def listed_tiles(r):
        return table_s[0, r], table_s[1, r]

    def tile_rows(ref, tile, count):
        return ref[pl.ds(tile, count, stride=plane_step), :].astype(bf16)

    def twice(value):
        return jnp.concatenate([value, value], axis=1)

    def side_by_side(value):
        return jnp.concatenate([value[0:size], value[size : 2 * size]], axis=1)

    def distances(u, one, two):
        def stacked(ref, tile):
            return ref[pl.ds(tile, KDEPTH, stride=plane_step), :]

        a = jnp.concatenate([stacked(side_a, one[0]), stacked(side_a, two[0])], axis=0)
        none = jnp.zeros((KDEPTH, size), f32)
        left = jnp.concatenate([stacked(side_b, one[1]), none], axis=0)
        right = jnp.concatenate([none, stacked(side_b, two[1])], axis=0)
        b = jnp.concatenate([left.astype(bf16), right.astype(bf16)], axis=1)
        both = lax.dot_general(
            a.astype(bf16), b, (((0,), (0,)), ((), ())), preferred_element_type=f32
        )
        squares[u] = both[:, 0:size]
        squares[u + 1] = both[:, size:]

    def weigh(r, u):
        square = lax.clamp(1e-13, squares[u], 1.0)
        fall = 1.0 - square * lax.rsqrt(square)
        fall2 = fall * fall
        falls[r] = fall
        weight_hi, weight_lo = split_in(fall2 * fall2 * (1.25 - fall), 2)
        weights[u, 0:size] = weight_hi
        weights[u, size : 2 * size] = weight_lo

    def add_up(r, u, t1, t2, cross):
        both = weights[u]
        got = dot_nt(twice(tile_rows(mass_rows, t2, 8)), side_by_side(both))
        row_density[pl.ds(r if cross else 2 * rows + r, 1)] = got[0:1] + got[1:2]
        if cross:
            got = dot_nn(twice(tile_rows(mass_rows, t1, 8)), both)
            row_density[pl.ds(rows + r, 1)] = got[0:1] + got[1:2]

    def density_rows(start, end, tiles_of, cross):
        for u in range(0, UNROLL, 2):
            distances(u, tiles_of(start + u), tiles_of(start + u + 1))

        def turn(step, carry):
            for u in range(UNROLL):
                r = start + step * UNROLL + u
                before = jnp.maximum(r - UNROLL, start)
                spare = jnp.where(step == 0, (2 * rows if cross else 0) + tiles + u, before)
                add_up(spare, u, *tiles_of(before), cross)
                weigh(r, u)
                if u % 2:
                    ahead = jnp.minimum(r + UNROLL, end - 1)
                    distances(u - 1, tiles_of(ahead - 1), tiles_of(ahead))
            return carry

        lax.fori_loop(0, (end - start) // UNROLL, turn, 0)
        for u in range(UNROLL):
            r = end - UNROLL + u
            add_up(r, u, *tiles_of(r), cross)

    def slopes(start, end):
        def turn(step, carry):
            for u in range(4):
                r = start + step * 4 + u
                fall = falls[r]
                slope_hi, slope_lo = split_in(fall * fall * fall, 2)
                slope[r, 0:size] = slope_hi
                slope[r, size : 2 * size] = slope_lo
            return carry

        lax.fori_loop(0, (end - start) // 4, turn, 0)

    def keep_sums(row, got):
        value = got[0:FEATURES] + got[FEATURES:]
        high, low = (piece.astype(f32) for piece in split_in(value, 2))
        force_high[pl.ds(row, FEATURES, stride=force_step), :] = high
        force_low[pl.ds(row, FEATURES, stride=force_step), :] = low

    def force_row(r, t1, t2, cross):
        both = slope[r]
        got = dot_nt(twice(tile_rows(feats, t2, 2 * FEATURES)), side_by_side(both))
        keep_sums(r if cross else 2 * rows + r, got)
        if cross:
            keep_sums(rows + r, dot_nn(twice(tile_rows(feats, t1, 2 * FEATURES)), both))

    def force_rows(start, end, tiles_of, cross, unroll=FORCE_UNROLL):
        def turn(step, carry):
            for u in range(unroll):
                r = start + step * unroll + u
                force_row(r, *tiles_of(r), cross)
            return carry

        lax.fori_loop(0, (end - start) // unroll, turn, 0)

    density_rows(0, tiles, own_tiles, False)
    slopes(0, tiles)
    table_copy.wait()
    for b in INWARD:
        arrived(0, b, pos_of)
        distance_planes(b)
    for b in INWARD:
        arrived(5, b, mass_of)
        mass_planes(b)
    for load in loads[4:6]:
        load.wait()
    sent.append(exchange(1, lambda b: vs.at[OWN], slot(vs)))
    density_rows(tiles, rows, listed_tiles, True)

    chosen = picks[...]
    total = jnp.zeros((all_tiles, size), f32)
    for part in split_in(row_density[0 : 2 * rows], 3):
        total = total + dot_nn(chosen, part)
    dens_part[...] = ((4.0 * kernel_norm) * total).reshape(BOXES, tiles, size)
    sent.append(exchange(2, lambda b: dens_part.at[b], slot(dens_recv)))
    slopes(tiles, 3 * rows // 4)
    for ref in (force_high, force_low):
        for f in range(12):
            for start in (0, rows):
                ref[pl.ds(f * force_step + start, tiles)] = jnp.zeros((tiles, size), f32)
    density = dens_part[OWN] + (4.0 * kernel_norm) * row_density[2 * rows : 2 * rows + tiles]
    for b in INWARD:
        arrived(2, b, slot(dens_recv))
        density = density + jnp.where(there[b], dens_recv[b], 0.0)
    dens_total[OWN] = density
    density_out[...] = density
    sent.append(exchange(3, lambda b: dens_total.at[OWN], slot(dens_total)))

    def pressures(b):
        density = dens_total[b]
        scale = density + 1.0 - jnp.where(pm[b, 3] > 0.0, 1.0, 0.0)
        inverse = 1.0 / scale
        press = vs[b, 3] * (density - rest_density) * inverse * inverse
        return press, inverse

    def force_planes(b):
        press, inverse = pressures(b)
        m = pm[b, 3]
        mp, mq = m * press, m * inverse
        values = [m] + [m * pm[b, c] for c in range(3)]
        values += [mp] + [mp * pm[b, c] for c in range(3)]
        values += [mq] + [mq * vs[b, c] for c in range(3)]
        for k, value in enumerate(values):
            for part, piece in enumerate(split_in(value, 2)):
                at_plane(feats, part * FEATURES + k, b)[...] = piece.astype(f32)

    slopes(3 * rows // 4, rows)
    force_planes(OWN)
    force_rows(0, tiles, own_tiles, False)
    for b in INWARD:
        arrived(1, b, slot(vs))
        arrived(3, b, slot(dens_total))
        force_planes(b)
    force_rows(tiles, rows, listed_tiles, True, 48)

    sums = []
    for f in range(0, 12, 2):
        total = jnp.zeros((all_tiles, 2 * size), f32)
        for ref in (force_high, force_low):
            pair = [ref[pl.ds((f + k) * force_step, 2 * rows)].astype(bf16) for k in range(2)]
            total = total + dot_nn(chosen, jnp.concatenate(pair, axis=1))
        sums += [total[:, 0:size], total[:, size:]]
    sent.append((4, lambda b: force_part.at[b], slot(force_recv)))
    for b in BESIDE + (OWN,):
        press, inverse = pressures(b)
        s = [v[b * tiles : (b + 1) * tiles] for v in sums]
        if b == OWN:
            for f in range(12):
                own = pl.ds(f * force_step + 2 * rows, tiles)
                s[f] = s[f] + force_high[own] + force_low[own]
        for c in range(3):
            h, v = pm[b, c], vs[b, c]
            push = press * (h * s[0] - s[1 + c]) + h * s[4] - s[5 + c]
            drag = inverse * (v * s[8] - s[9 + c])
            force_part[b, c] = (5.0 * kernel_norm) * (2.0 * push - (2.0 * viscosity) * drag)
        if b != OWN:
            send_to(4, b, force_part.at[b], slot(force_recv))
    accel = force_part[OWN]
    for b in INWARD:
        arrived(4, b, slot(force_recv))
        accel = accel + jnp.where(there[b], force_recv[b], 0.0)
    accel = accel * jnp.where(pm[OWN, 3] > 0.0, 1.0, 0.0)[None]
    new_speeds = vs[OWN, 0:3] + time_step * accel
    speeds_out[...] = new_speeds
    points_out[...] = pos[...] + time_step * new_speeds

    for stage, source_of, target in sent:
        for b in BESIDE:

            @pl.when(there[b])
            def _(b=b):
                copy_to(stage, b, source_of(b), target).wait_send()


def store_kernel(points, speeds, density, points_out, speeds_out, density_out, sem):
    pairs = ((points, points_out), (speeds, speeds_out), (density, density_out))
    stores = [pltpu.make_async_copy(a, b, sem.at[k]) for k, (a, b) in enumerate(pairs)]
    for store in stores:
        store.start()
    for store in stores:
        store.wait()


def body(gx, gy, positions, velocities, mass, stiffness, counts, pairs, pair_count):
    tiles = counts.shape[2]
    size = positions.shape[3] // tiles
    rows = pairs.shape[0]
    all_tiles = BOXES * tiles
    points = positions.reshape(3, tiles, size)
    speeds = velocities.reshape(3, tiles, size)
    turned = pairs.T
    vmem = pl.BlockSpec(memory_space=pltpu.VMEM)
    hbm = pl.BlockSpec(memory_space=pltpu.HBM)
    shapes = (
        jax.ShapeDtypeStruct((3, tiles, size), f32),
        jax.ShapeDtypeStruct((3, tiles, size), f32),
        jax.ShapeDtypeStruct((tiles, size), f32),
    )
    results = pl.pallas_call(
        functools.partial(kernel, gx, gy, tiles, size, rows),
        out_shape=shapes,
        in_specs=[hbm] * 6 + [pl.BlockSpec(memory_space=pltpu.SMEM)],
        out_specs=(vmem,) * 3,
        scratch_shapes=[
            pltpu.VMEM((3, tiles, size), f32),
            pltpu.VMEM((tiles, size), f32),
            pltpu.VMEM((1, tiles), jnp.int32),
            pltpu.VMEM((2, rows), jnp.int32),
            pltpu.SemaphoreType.DMA((6,)),
            pltpu.VMEM((BOXES, 4, tiles, size), f32),
            pltpu.VMEM((BOXES, 4, tiles, size), f32),
            pltpu.VMEM((KDEPTH * (all_tiles + 1), size), f32),
            pltpu.VMEM((KDEPTH * (all_tiles + 1), size), f32),
            pltpu.VMEM((8 * (all_tiles + 1), size), f32),
            pltpu.VMEM((2 * FEATURES * (all_tiles + 1), size), f32),
            pltpu.VMEM((UNROLL, size, size), f32),
            pltpu.VMEM((UNROLL, 2 * size, size), bf16),
            pltpu.VMEM((rows, size, size), f32),
            pltpu.VMEM((rows, 2 * size, size), bf16),
            pltpu.VMEM((3 * rows + 2 * tiles + 16, size), f32),
            pltpu.VMEM((FEATURES * (2 * rows + tiles + 1), size), f32),
            pltpu.VMEM((FEATURES * (2 * rows + tiles + 1), size), f32),
            pltpu.VMEM((all_tiles, 2 * rows), bf16),
            pltpu.VMEM((2, rows), jnp.int32),
            pltpu.SMEM((2, rows), jnp.int32),
            pltpu.SemaphoreType.DMA,
            pltpu.VMEM((BOXES, tiles, size), f32),
            pltpu.VMEM((BOXES, tiles, size), f32),
            pltpu.VMEM((BOXES, tiles, size), f32),
            pltpu.VMEM((BOXES, 3, tiles, size), f32),
            pltpu.VMEM((BOXES, 3, tiles, size), f32),
            pltpu.SemaphoreType.DMA((6, BOXES)),
            pltpu.SemaphoreType.DMA((6, BOXES)),
        ],
        compiler_params=pltpu.CompilerParams(collective_id=0, has_side_effects=True, vmem_limit_bytes=40 << 20),
        name="sph_step",
    )(
        *(
            pltpu.with_memory_space_constraint(value, pltpu.HBM)
            for value in (
                points,
                speeds,
                mass.reshape(tiles, size),
                stiffness.reshape(tiles, size),
                counts.reshape(1, tiles),
                turned,
            )
        ),
        pair_count,
    )
    new_points, new_speeds, density = pl.pallas_call(
        store_kernel,
        out_shape=shapes,
        in_specs=[vmem] * 3,
        out_specs=(hbm,) * 3,
        scratch_shapes=[pltpu.SemaphoreType.DMA((3,))],
        compiler_params=pltpu.CompilerParams(vmem_limit_bytes=1 << 20),
        name="sph_store",
    )(*results)
    return (
        new_points.reshape(positions.shape),
        new_speeds.reshape(velocities.shape),
        density.reshape(mass.shape),
    )


def solution(mesh):
    placed = (
        P(None, "gx", "gy", None),
        P(None, "gx", "gy", None),
        P("gx", "gy", None),
        P("gx", "gy", None),
        P("gx", "gy", None),
        P(("gx", "gy"), None),
        P(("gx", "gy")),
    )
    return jax.shard_map(
        functools.partial(body, mesh.shape["gx"], mesh.shape["gy"]),
        mesh=mesh,
        in_specs=placed,
        out_specs=(P(None, "gx", "gy", None), P(None, "gx", "gy", None), P("gx", "gy", None)),
        check_vma=False,
    )
```
